256 devices in a mesh: view: 8 (over y_lo, x), tile: 32 (over y_hi, z, core).
Axes of the slice: x: 4, y: 4 (y_hi: 2, y_lo: 2; y = y_hi * 2 + y_lo), z: 8, core: 2. Of those that a mesh axis runs over, the one named last changes fastest.
Arguments:
- estimate: float32 [1024, 64, 256], P('tile'), may hold values from 0.5 to 2
- measured: bfloat16 [8, 1024, 64, 256], P('view', 'tile'), may hold values from 0.5 to 2
- blur_profile: float32 [8, 256], P('view'), may hold values from 0.1 to 1
- view_offset: int32 [8], P('view'), may hold values from -6 to 6, as said below
- tile_shift: int32 [8], P('view'), may hold values from 0 to 31
Outputs:
- updated: float32 [1024, 64, 256], P('tile')
The draws below stay inside these ranges and needn't reach their ends.
Inputs may be any that keep to these rules, and one draw needn't show every extreme that they name: `view_offset`: some view has offset 6 and some other view has offset -6.
All inputs are finite; a program needn't handle non-finite values.
Results may differ from the reference program's by a relative error of at most 0.0016.
Values may be sent and summed in bfloat16 or wider, within the bound.
No kernel may reach another device: no remote copies, remote signals or barrier semaphores. Data moves between devices by JAX's collectives and lax.ppermute only.
A program may use at most 64 MiB of HBM per device.

```python
import math
import jax
import jax.numpy as jnp

CX = 32
CY = 64
CZ = 256
H = 6
VIEWS = 8
NX = 1024
N_TILE = 32


def draw_view_offset(key, part):
    offsets = jax.random.randint(key, (VIEWS,), -H, H + 1)
    chosen_views = jax.random.permutation(jax.random.fold_in(key, 7), VIEWS)
    offsets = offsets.at[chosen_views[0]].set(H)
    offsets = offsets.at[chosen_views[1]].set(-H)
    return offsets.astype(jnp.int32)


def draw_measured(key, part):
    shape = (VIEWS, NX, CY, CZ)
    exponent = jax.random.uniform(key, shape, jnp.float32, math.log(0.5), math.log(2.0))
    values = jnp.exp(exponent)
    return jnp.clip(values, 0.5, 2.0).astype(jnp.bfloat16)


def with_ends(result, rng, low, top_value):
    spot = [jax.random.randint(jax.random.fold_in(rng, axis), (), 0, length) for axis, length in enumerate(result.shape)]
    main_axis = result.shape.index(max(result.shape))
    beside = spot[:main_axis] + [(spot[main_axis] + 1) % result.shape[main_axis]] + spot[main_axis + 1:]
    return result.at[tuple(spot)].set(low).at[tuple(beside)].set(top_value)


def shard_levels(rng, extent, pieces, smallest, largest):
    factor_of, own = 1.0, jax.random.fold_in(rng, 6)
    for dim, blocks in pieces:
        heights = jnp.exp(jax.random.uniform(jax.random.fold_in(own, dim), (blocks,), jnp.float32, smallest / len(pieces), largest / len(pieces)))
        factor_of = factor_of * jnp.repeat(heights, extent[dim] // blocks).reshape([-1 if axis == dim else 1 for axis in range(len(extent))])
    return factor_of


def setup_inputs(seed: int = 0) -> dict:
    keys = jax.random.split(jax.random.key(seed), 6)
    return {
        "estimate": jnp.clip(jnp.exp(math.log(2.0) - 1.3862944 * jax.random.uniform(keys[0], (NX, CY, CZ), jnp.float32) ** shard_levels(keys[0], (NX, CY, CZ), ((0, 32),), -0.2, 0.2)), 0.5, 2.0),
        "measured": draw_measured(jax.random.fold_in(keys[5], 71), 0),
        "blur_profile": jnp.clip(jnp.exp(math.log(1.0) - 2.3025851 * jax.random.uniform(keys[2], (VIEWS, CZ), jnp.float32) ** shard_levels(keys[2], (VIEWS, CZ), ((0, 8),), -0.2, 0.2)), 0.1, 1.0),
        "view_offset": draw_view_offset(jax.random.fold_in(keys[5], 71), 0),
        "tile_shift": with_ends(jax.random.randint(keys[4], (VIEWS,), 0, N_TILE), jax.random.fold_in(keys[4], 1), 0, N_TILE - 1).astype(jnp.int32),
    }


profile_sigma = 48.0


def make_kernel(profile):
    length = profile.shape[0]
    column = jnp.arange(length)
    distance = jnp.minimum(column, length - column).astype(jnp.float32)
    weights = profile * jnp.exp(-distance * distance / (2.0 * profile_sigma * profile_sigma))
    return weights / jnp.sum(weights)


def reference(estimate, measured, blur_profile, view_offset, tile_shift):
    log_total = jnp.zeros(estimate.shape, jnp.float32)
    for view_index in range(VIEWS):
        kernel = make_kernel(blur_profile[view_index])
        spectrum = jnp.fft.fft(kernel)
        blend_weight = (view_index + 1) / (VIEWS + 1)
        travel = tile_shift[view_index] * CX + view_offset[view_index]
        warped = blend_weight * jnp.roll(estimate, -travel, axis=0) + (1 - blend_weight) * jnp.roll(estimate, -travel - 1, axis=0)
        forward = jnp.real(jnp.fft.ifft(jnp.fft.fft(warped, axis=-1) * spectrum, axis=-1)).astype(jnp.float32)
        ratios = measured[view_index].astype(jnp.float32) / forward
        back = jnp.real(jnp.fft.ifft(jnp.fft.fft(ratios, axis=-1) * jnp.conj(spectrum), axis=-1)).astype(jnp.float32)
        correction = blend_weight * jnp.roll(back, travel, axis=0) + (1 - blend_weight) * jnp.roll(back, travel + 1, axis=0)
        log_total = log_total + jnp.log(correction)
    return estimate * jnp.exp(log_total)
```

```python
import functools

import jax
import jax.numpy as jnp
from jax import lax
from jax.experimental import pallas as pl
from jax.experimental.pallas import tpu as pltpu
from jax.sharding import PartitionSpec as P

PROFILE_SIGMA = 48.0
CORR_MID = 2.125
CORR_SCALE = 32700.0 / 1.9
LOG_SCALE = 32700.0 / 11.2


def encode(value):
    whole = jnp.floor(jnp.clip(value, -32767.0, 32767.0) + 0.5)
    return whole.astype(jnp.int32).astype(jnp.int16)


def decode(code):
    return code.astype(jnp.int32).astype(jnp.float32)


def blur_matrix(profile):
    length = profile.shape[1]
    column = lax.broadcasted_iota(jnp.int32, (8, length), 1)
    distance = jnp.minimum(column, length - column).astype(jnp.float32)
    weights = profile * jnp.exp(-distance * distance / (2.0 * PROFILE_SIGMA * PROFILE_SIGMA))
    kernel = weights / jnp.sum(weights, axis=1, keepdims=True)
    rows = jnp.broadcast_to(kernel[:1], (length, length))
    return pltpu.roll(rows, 0, 1, stride=1, stride_axis=0)


def view_kernel(move_ref, blend_ref, profile_ref, meas_ref, est_ref, out_ref, e_ref, m_ref, b_ref):
    slabs, rows = 32, 32
    total = slabs * rows
    shift, offset = move_ref[0], move_ref[1]
    a = blend_ref[0]
    b = 1.0 - a
    skip = lax.div(8 - offset, 8)
    turn = lax.rem(40 - (8 - offset - 8 * skip), 40)
    matrix = blur_matrix(profile_ref[...]).astype(jnp.bfloat16)

    def one_line(line, carry):
        def fill(t, c):
            base = pl.multiple_of(t * rows, rows)
            for h in range(2):
                lanes = pl.ds(128 * h, 128)
                for g in range(4):
                    e_ref[pl.ds(base + 8 * g, 8), lanes] = est_ref[
                        h * 4 + g, 2 * t + line
                    ].astype(jnp.float32)
                m_ref[pl.ds(base + 8, rows), lanes] = meas_ref[
                    2 * t + line, pl.ds(32 * h, 32)
                ].astype(jnp.float32)
            return c

        lax.fori_loop(0, slabs, fill, 0)
        e_ref[pl.ds(total, 8)] = e_ref[pl.ds(0, 8)]
        m_ref[pl.ds(0, 8)] = m_ref[pl.ds(total, 8)]
        m_ref[pl.ds(total + 8, 8)] = m_ref[pl.ds(8, 8)]

        group = 4

        def blur(k, c):
            base = pl.multiple_of(k * (rows * group), rows * group)
            wide = e_ref[pl.ds(base, rows * group + 8)]
            warped = a * wide[: rows * group] + b * wide[1 : rows * group + 1]
            warped = warped.astype(jnp.bfloat16)
            forward = jnp.dot(warped, matrix, preferred_element_type=jnp.float32)
            parts = []
            for q in range(group):
                t = lax.rem(k * group + q - shift + 2 * slabs, slabs)
                start = pl.multiple_of(t * rows + 8 * skip, 8)
                wide = m_ref[pl.ds(start, rows + 8)]
                parts.append(pltpu.roll(wide, turn, 0)[:rows])
            ratios = (jnp.concatenate(parts, axis=0) / forward).astype(jnp.bfloat16)
            back = lax.dot_general(
                ratios, matrix, (((1,), (1,)), ((), ())), preferred_element_type=jnp.float32
            )
            b_ref[pl.ds(base + 8, rows * group)] = back
            return c

        lax.fori_loop(0, slabs // group, blur, 0)
        b_ref[pl.ds(0, 8)] = b_ref[pl.ds(total, 8)]

        def join(s, c):
            base = pl.multiple_of(s * rows, rows)
            wide = b_ref[pl.ds(base, rows + 8)]
            correction = a * wide[8:] + b * wide[7 : rows + 7]
            code = encode((correction - CORR_MID) * CORR_SCALE)
            for h in range(2):
                for g in range(4):
                    out_ref[h * 4 + g, 2 * s + line] = code[8 * g : 8 * g + 8, 128 * h : 128 * h + 128]
            return c

        lax.fori_loop(0, slabs, join, 0)
        return carry

    lax.fori_loop(0, 2, one_line, 0)


def final_kernel(est_ref, code_ref, out_ref):
    for h in range(2):
        lanes = pl.ds(128 * h, 128)
        factor = jnp.exp(decode(code_ref[h, 0]) * (1.0 / LOG_SCALE))
        out_ref[:, :, lanes] = est_ref[:, :, lanes] * factor


VMEM = pl.BlockSpec(memory_space=pltpu.VMEM)
SMEM = pl.BlockSpec(memory_space=pltpu.SMEM)


def body(estimate, measured, blur_profile, view_offset, tile_shift):
    views = lax.axis_size("view")
    view = lax.axis_index("view")
    blend = (view + 1).astype(jnp.float32) / (views + 1)
    group, half = view % 4, view // 4

    piece = lax.dynamic_slice(estimate, (8 * group, 0, 128 * half), (8, 64, 128))
    piece = piece.astype(jnp.bfloat16).transpose(1, 0, 2)
    image = measured[0].reshape(32, 64, 2, 128).transpose(1, 2, 0, 3).reshape(64, 64, 128)
    send = jnp.concatenate([image, piece], axis=1)
    lines = lax.all_to_all(send, "tile", 0, 0, tiled=True)

    piece = jnp.broadcast_to(lines[None, :, 64:], (8, 64, 8, 128))
    est_lines = lax.all_to_all(piece, "view", 0, 0, tiled=True)

    codes = pl.pallas_call(
        view_kernel,
        out_shape=jax.ShapeDtypeStruct((8, 64, 8, 128), jnp.int16),
        in_specs=[SMEM, SMEM, VMEM, VMEM, VMEM],
        out_specs=VMEM,
        scratch_shapes=[
            pltpu.VMEM((1032, 256), jnp.float32),
            pltpu.VMEM((1040, 256), jnp.float32),
            pltpu.VMEM((1032, 256), jnp.float32),
        ],
        name="view_kernel",
    )(
        jnp.stack([tile_shift[0], view_offset[0]]),
        blend.reshape(1),
        jnp.broadcast_to(blur_profile, (8, 256)),
        lines,
        est_lines,
    )
    codes = lax.all_to_all(codes, "view", 0, 0, tiled=True)
    product = jnp.prod(decode(codes) * (1.0 / CORR_SCALE) + CORR_MID, axis=0)
    logs = encode(jnp.log(product) * LOG_SCALE)
    logs = lax.all_to_all(logs, "tile", 0, 0, tiled=True)
    logs = jnp.broadcast_to(logs.transpose(1, 0, 2)[None], (8, 8, 64, 128))
    logs = lax.all_to_all(logs, "view", 0, 0, tiled=True)

    return pl.pallas_call(
        final_kernel,
        grid=(4,),
        out_shape=jax.ShapeDtypeStruct((32, 64, 256), jnp.float32),
        in_specs=[
            pl.BlockSpec((8, 64, 256), lambda g: (g, 0, 0)),
            pl.BlockSpec((2, 1, 8, 64, 128), lambda g: (0, g, 0, 0, 0)),
        ],
        out_specs=pl.BlockSpec((8, 64, 256), lambda g: (g, 0, 0)),
        name="final_kernel",
    )(estimate, logs.reshape(2, 4, 8, 64, 128))


def solution(mesh):
    placed = (
        P("tile", None, None),
        P("view", "tile", None, None),
        P("view", None),
        P("view"),
        P("view"),
    )
    return jax.shard_map(
        body, mesh=mesh, in_specs=placed, out_specs=P("tile", None, None), check_vma=False
    )
```

```python
import jax
import jax.numpy as jnp
from jax import lax
from jax.experimental import pallas as pl
from jax.experimental.pallas import tpu as pltpu
from jax.sharding import Mesh, PartitionSpec as P

PROFILE_SIGMA = 48.0
PAIR_SCALE = 32700.0 / 2.8
TOTAL_SCALE = PAIR_SCALE / 4.0
SLABS, ROWS, LENGTH = 32, 32, 256
TOTAL = SLABS * ROWS


def blur_matrix(profile):
    column = lax.broadcasted_iota(jnp.int32, (1, LENGTH), 1)
    distance = jnp.minimum(column, LENGTH - column).astype(jnp.float32)
    weights = profile * jnp.exp(-distance * distance / (2.0 * PROFILE_SIGMA * PROFILE_SIGMA))
    kernel = weights / jnp.sum(weights, axis=1, keepdims=True)
    rows = jnp.broadcast_to(kernel, (LENGTH, LENGTH))
    return pltpu.roll(rows, 0, 1, stride=1, stride_axis=0)


def pair_kernel(
    place_ref, own_ref, other_ref, own_profile_ref, other_profile_ref, data_ref, out_ref,
    e_ref, m_ref, b_ref,
):
    upper = place_ref[0]
    column = place_ref[1]

    def fill_estimate(t, c):
        base = pl.multiple_of(t * ROWS, ROWS)
        for h in range(2):
            e_ref[pl.ds(base, ROWS), pl.ds(128 * h, 128)] = data_ref[
                h * SLABS + t, pl.ds(64, ROWS)
            ].astype(jnp.float32)
        return c

    lax.fori_loop(0, SLABS, fill_estimate, 0)
    e_ref[pl.ds(TOTAL, 8)] = e_ref[pl.ds(0, 8)]
    group = 4
    row = lax.broadcasted_iota(jnp.int32, (1, 8, LENGTH), 1)

    blends = []
    for w in range(2):
        is_own = upper == w
        shift = jnp.where(is_own, own_ref[0], other_ref[0])
        offset = jnp.where(is_own, own_ref[1], other_ref[1])
        a = (w * 4 + column + 1).astype(jnp.float32) / 9.0
        b = 1.0 - a
        blends.append((a, b))
        skip = lax.div(8 - offset, 8)
        rest = 8 - offset - 8 * skip
        turn = lax.rem(8 - rest, 8)
        profile = jnp.where(is_own, own_profile_ref[...], other_profile_ref[...])
        matrix = blur_matrix(profile).astype(jnp.bfloat16)

        def fill_image(t, c, w=w):
            base = pl.multiple_of(t * ROWS, ROWS)
            for h in range(2):
                m_ref[pl.ds(base + 8, ROWS), pl.ds(128 * h, 128)] = data_ref[
                    w * SLABS + t, pl.ds(32 * h, ROWS)
                ].astype(jnp.float32)
            return c

        lax.fori_loop(0, SLABS, fill_image, 0)
        m_ref[pl.ds(0, 8)] = m_ref[pl.ds(TOTAL, 8)]
        m_ref[pl.ds(TOTAL + 8, 8)] = m_ref[pl.ds(8, 8)]

        def blur(k, c, w=w, a=a, b=b, matrix=matrix, skip=skip, rest=rest, turn=turn, shift=shift):
            base = pl.multiple_of(k * (ROWS * group), ROWS * group)
            wide = e_ref[pl.ds(base, ROWS * group + 8)]
            warped = a * wide[: ROWS * group] + b * wide[1 : ROWS * group + 1]
            warped = warped.astype(jnp.bfloat16)
            forward = jnp.dot(warped, matrix, preferred_element_type=jnp.float32)
            parts = []
            for q in range(group):
                t = lax.rem(k * group + q - shift + 2 * SLABS, SLABS)
                start = pl.multiple_of(t * ROWS + 8 * skip, 8)
                tiles = m_ref[pl.ds(start, ROWS + 8)].reshape(5, 8, LENGTH)
                tiles = pltpu.roll(tiles, turn, 1)
                part = jnp.where(row < 8 - rest, tiles[:4], tiles[1:])
                parts.append(part.reshape(ROWS, LENGTH))
            ratios = (jnp.concatenate(parts, axis=0) / forward).astype(jnp.bfloat16)
            back = lax.dot_general(
                ratios, matrix, (((1,), (1,)), ((), ())), preferred_element_type=jnp.float32
            )
            b_ref[w, pl.ds(base + 8, ROWS * group)] = back
            return c

        lax.fori_loop(0, SLABS // group, blur, 0)
        b_ref[w, pl.ds(0, 8)] = b_ref[w, pl.ds(TOTAL, 8)]

    def join(s, c):
        base = pl.multiple_of(s * ROWS, ROWS)
        product = None
        for w, (a, b) in enumerate(blends):
            wide = b_ref[w, pl.ds(base, ROWS + 8)]
            correction = a * wide[8:] + b * wide[7 : ROWS + 7]
            product = correction if product is None else product * correction
        code = jnp.clip(jnp.log(product) * PAIR_SCALE, -32767.0, 32767.0)
        code = jnp.floor(code + 0.5).astype(jnp.int32).astype(jnp.int16)
        for g in range(4):
            out_ref[g, s] = code[8 * g : 8 * g + 8]
        return c

    lax.fori_loop(0, SLABS, join, 0)


def final_kernel(est_ref, code_ref, out_ref):
    for h in range(2):
        lines = pl.ds(32 * h, 32)
        logs = code_ref[h, 0].astype(jnp.int32).astype(jnp.float32) * (1.0 / TOTAL_SCALE)
        out_ref[:, lines] = est_ref[:, lines] * jnp.exp(logs)


VMEM = pl.BlockSpec(memory_space=pltpu.VMEM)
SMEM = pl.BlockSpec(memory_space=pltpu.SMEM)


def body(estimate, measured, blur_profile, view_offset, tile_shift):
    upper = lax.axis_index("upper")
    column = lax.axis_index("column")
    swap = [(0, 1), (1, 0)]
    moves = jnp.concatenate([tile_shift, view_offset])
    other_moves = lax.ppermute(moves, "upper", swap)
    other_profile = lax.ppermute(blur_profile, "upper", swap)

    piece = lax.dynamic_slice(estimate, (0, 0, 128 * upper), (32, 64, 128))
    piece = piece.astype(jnp.bfloat16).transpose(1, 0, 2)
    image = measured[0].reshape(32, 64, 2, 128).transpose(1, 2, 0, 3).reshape(64, 64, 128)
    send = jnp.concatenate([image, piece], axis=1)
    data = lax.all_to_all(send, ("upper", "tile"), 0, 0, tiled=True)

    codes = pl.pallas_call(
        pair_kernel,
        out_shape=jax.ShapeDtypeStruct((4, SLABS, 8, LENGTH), jnp.int16),
        in_specs=[SMEM, SMEM, SMEM, VMEM, VMEM, VMEM],
        out_specs=VMEM,
        scratch_shapes=[
            pltpu.VMEM((TOTAL + 8, LENGTH), jnp.float32),
            pltpu.VMEM((TOTAL + 16, LENGTH), jnp.float32),
            pltpu.VMEM((2, TOTAL + 8, LENGTH), jnp.float32),
        ],
        name="pair_kernel",
    )(
        jnp.stack([upper, column]),
        moves,
        other_moves,
        blur_profile,
        other_profile,
        data,
    )
    codes = lax.all_to_all(codes, "column", 0, 0, tiled=True)
    total = jnp.sum(codes.astype(jnp.int32), axis=0)
    logs = ((total + 2) >> 2).astype(jnp.int16)
    logs = lax.all_to_all(logs, "tile", 0, 0, tiled=True)
    logs = jnp.broadcast_to(logs.transpose(1, 0, 2)[None], (8, 8, 32, LENGTH))
    logs = lax.all_to_all(logs, ("upper", "column"), 0, 0, tiled=True)

    return pl.pallas_call(
        final_kernel,
        grid=(4,),
        out_shape=jax.ShapeDtypeStruct((32, 64, LENGTH), jnp.float32),
        in_specs=[
            pl.BlockSpec((8, 64, LENGTH), lambda g: (g, 0, 0)),
            pl.BlockSpec((2, 1, 8, 32, LENGTH), lambda g: (0, g, 0, 0, 0)),
        ],
        out_specs=pl.BlockSpec((8, 64, LENGTH), lambda g: (g, 0, 0)),
        name="final_kernel",
    )(estimate, logs.reshape(2, 4, 8, 32, LENGTH))


def solution(mesh):
    fine = Mesh(mesh.devices.reshape(2, 4, 32), ("upper", "column", "tile"))
    view = ("upper", "column")
    placed = (P("tile"), P(view, "tile"), P(view), P(view), P(view))
    return jax.shard_map(
        body, mesh=fine, in_specs=placed, out_specs=P("tile"), check_vma=False
    )
```

```python
import jax
import jax.numpy as jnp
from jax import lax
from jax.experimental import pallas as pl
from jax.experimental.pallas import tpu as pltpu
from jax.sharding import Mesh, PartitionSpec as P

PROFILE_SIGMA = 48.0
PAIR_SCALE = 32700.0 / 2.8
TOTAL_SCALE = PAIR_SCALE / 4.0
SLABS, ROWS, LENGTH = 32, 32, 256
TOTAL = SLABS * ROWS
GROUP = 4


def blur_matrix(profile):
    column = lax.broadcasted_iota(jnp.int32, (1, LENGTH), 1)
    distance = jnp.minimum(column, LENGTH - column).astype(jnp.float32)
    weights = profile * jnp.exp(-distance * distance / (2.0 * PROFILE_SIGMA * PROFILE_SIGMA))
    kernel = weights / jnp.sum(weights, axis=1, keepdims=True)
    rows = jnp.broadcast_to(kernel, (LENGTH, LENGTH))
    return pltpu.roll(rows, 0, 1, stride=1, stride_axis=0)


def tile_rows(wide, rest, turn, row):
    tiles = pltpu.roll(wide.reshape(-1, 8, LENGTH), turn, 1)
    count = tiles.shape[0]
    tiles = jnp.where(row < 8 - rest, tiles[: count - 1], tiles[1:])
    return tiles.reshape(8 * count - 8, LENGTH)


def blend_of(column, w):
    a = (w * 4 + column + 1).astype(jnp.float32) / 9.0
    return a, 1.0 - a


def forward_kernel(
    place_ref, own_ref, other_ref, own_profile_ref, other_profile_ref, est0_ref, est1_ref,
    est2_ref, est3_ref, inverse_ref, matrix_ref, e_ref,
):
    est_refs = (est0_ref, est1_ref, est2_ref, est3_ref)
    upper, column = place_ref[0], place_ref[1]

    def fill(t, c):
        for d, est_ref in enumerate(est_refs):
            first = t * ROWS + 8 * lax.rem(column + 4 - d, 4) + 8
            e_ref[pl.ds(pl.multiple_of(first, 8), 8)] = est_ref[t].astype(jnp.float32)
        return c

    lax.fori_loop(0, SLABS, fill, 0)
    e_ref[pl.ds(0, 8)] = e_ref[pl.ds(TOTAL, 8)]
    e_ref[pl.ds(TOTAL + 8, 16)] = e_ref[pl.ds(8, 16)]
    row = lax.broadcasted_iota(jnp.int32, (1, 8, LENGTH), 1)

    for w in range(2):
        is_own = upper == w
        shift = jnp.where(is_own, own_ref[0], other_ref[0])
        offset = jnp.where(is_own, own_ref[1], other_ref[1])
        a, b = blend_of(column, w)
        skip = lax.div(8 + offset, 8)
        rest = 8 + offset - 8 * skip
        turn = lax.rem(8 - rest, 8)
        profile = jnp.where(is_own, own_profile_ref[...], other_profile_ref[...])
        matrix = blur_matrix(profile).astype(jnp.bfloat16)
        matrix_ref[w] = matrix

        def blur(k, c, w=w, a=a, b=b, matrix=matrix, skip=skip, rest=rest, turn=turn, shift=shift):
            base = pl.multiple_of(k * (ROWS * GROUP), ROWS * GROUP)
            parts = []
            for q in range(GROUP):
                s = lax.rem(k * GROUP + q + shift, SLABS)
                start = pl.multiple_of(s * ROWS + 8 * skip, 8)
                wide = tile_rows(e_ref[pl.ds(start, ROWS + 16)], rest, turn, row)
                parts.append(a * wide[:ROWS] + b * wide[1 : ROWS + 1])
            warped = jnp.concatenate(parts, axis=0).astype(jnp.bfloat16)
            forward = jnp.dot(warped, matrix, preferred_element_type=jnp.float32)
            inverse_ref[w, pl.ds(base, ROWS * GROUP)] = 1.0 / forward
            return c

        lax.fori_loop(0, SLABS // GROUP, blur, 0)


def back_kernel(
    place_ref, own_ref, other_ref, image_ref, inverse_ref, matrix_ref, out_ref, b_ref
):
    upper, column = place_ref[0], place_ref[1]
    row = lax.broadcasted_iota(jnp.int32, (1, 8, LENGTH), 1)

    for w in range(2):

        def blur(k, c, w=w):
            base = pl.multiple_of(k * (ROWS * GROUP), ROWS * GROUP)
            image = image_ref[pl.ds(w * SLABS + k * GROUP, GROUP)].reshape(ROWS * GROUP, LENGTH)
            ratios = image.astype(jnp.float32) * inverse_ref[w, pl.ds(base, ROWS * GROUP)]
            b_ref[w, pl.ds(base + 16, ROWS * GROUP)] = lax.dot_general(
                ratios.astype(jnp.bfloat16),
                matrix_ref[w],
                (((1,), (1,)), ((), ())),
                preferred_element_type=jnp.float32,
            )
            return c

        lax.fori_loop(0, SLABS // GROUP, blur, 0)
        b_ref[w, pl.ds(0, 16)] = b_ref[w, pl.ds(TOTAL, 16)]
        b_ref[w, pl.ds(TOTAL + 16, 8)] = b_ref[w, pl.ds(16, 8)]

    views = []
    for w in range(2):
        is_own = upper == w
        shift = jnp.where(is_own, own_ref[0], other_ref[0])
        offset = jnp.where(is_own, own_ref[1], other_ref[1])
        skip = lax.div(8 - offset, 8)
        rest = 8 - offset - 8 * skip
        views.append((shift, skip, rest, lax.rem(8 - rest, 8), *blend_of(column, w)))

    def join(s, c):
        product = None
        for w, (shift, skip, rest, turn, a, b) in enumerate(views):
            t = lax.rem(s - shift + SLABS, SLABS)
            start = pl.multiple_of(t * ROWS + 8 * skip, 8)
            wide = b_ref[w, pl.ds(start, ROWS + 16)]
            blended = a * wide[8:] + b * wide[7 : ROWS + 15]
            correction = tile_rows(blended, rest, turn, row)
            product = correction if product is None else product * correction
        code = jnp.clip(jnp.log(product) * PAIR_SCALE, -32767.0, 32767.0)
        code = jnp.floor(code + 0.5).astype(jnp.int32).astype(jnp.int16)
        for g in range(4):
            out_ref[g, s] = code[8 * g : 8 * g + 8]
        return c

    lax.fori_loop(0, SLABS, join, 0)


def final_kernel(est_ref, code_ref, out_ref):
    for h in range(2):
        lines = pl.ds(32 * h, 32)
        logs = code_ref[h, 0].astype(jnp.int32).astype(jnp.float32) * (1.0 / TOTAL_SCALE)
        out_ref[:, lines] = est_ref[:, lines] * jnp.exp(logs)


VMEM = pl.BlockSpec(memory_space=pltpu.VMEM)
SMEM = pl.BlockSpec(memory_space=pltpu.SMEM)


def body(estimate, measured, blur_profile, view_offset, tile_shift):
    upper = lax.axis_index("upper")
    column = lax.axis_index("column")
    swap = [(0, 1), (1, 0)]
    moves = jnp.concatenate([tile_shift, view_offset])
    other_moves = lax.ppermute(moves, "upper", swap)
    other_profile = lax.ppermute(blur_profile, "upper", swap)

    piece = lax.dynamic_slice(estimate, (8 * column, 32 * upper, 0), (8, 32, LENGTH))
    piece = piece.astype(jnp.bfloat16).transpose(1, 0, 2)
    piece = lax.all_to_all(piece, "tile", 0, 0, tiled=True)
    image = measured[0].transpose(1, 0, 2)
    image_lines = lax.all_to_all(image, ("upper", "tile"), 0, 0, tiled=True)
    est_lines = [piece]
    for d in (1, 2, 3):
        route = [(i, (i + d) % 4) for i in range(4)]
        est_lines.append(lax.ppermute(piece, "column", route))

    place = jnp.stack([upper, column])
    inverse, matrices = pl.pallas_call(
        forward_kernel,
        out_shape=(
            jax.ShapeDtypeStruct((2, TOTAL, LENGTH), jnp.float32),
            jax.ShapeDtypeStruct((2, LENGTH, LENGTH), jnp.bfloat16),
        ),
        in_specs=[SMEM] * 3 + [VMEM] * 6,
        out_specs=(VMEM, VMEM),
        scratch_shapes=[pltpu.VMEM((TOTAL + 24, LENGTH), jnp.float32)],
        cost_estimate=pl.CostEstimate(
            flops=4 * TOTAL * LENGTH * LENGTH, bytes_accessed=8 << 20, transcendentals=0
        ),
        compiler_params=pltpu.CompilerParams(vmem_limit_bytes=16 << 20),
        name="forward_kernel",
    )(place, moves, other_moves, blur_profile, other_profile, *est_lines)
    codes = pl.pallas_call(
        back_kernel,
        out_shape=jax.ShapeDtypeStruct((4, SLABS, 8, LENGTH), jnp.int16),
        in_specs=[SMEM, SMEM, SMEM, VMEM, VMEM, VMEM],
        out_specs=VMEM,
        scratch_shapes=[pltpu.VMEM((2, TOTAL + 24, LENGTH), jnp.float32)],
        compiler_params=pltpu.CompilerParams(vmem_limit_bytes=16 << 20),
        name="back_kernel",
    )(place, moves, other_moves, image_lines, inverse, matrices)
    codes = lax.all_to_all(codes, "column", 0, 0, tiled=True)
    total = jnp.sum(codes.astype(jnp.int32), axis=0)
    logs = ((total + 2) >> 2).astype(jnp.int16)
    logs = lax.all_to_all(logs, "tile", 0, 0, tiled=True)
    logs = jnp.broadcast_to(logs.transpose(1, 0, 2)[None], (8, 8, 32, LENGTH))
    logs = lax.all_to_all(logs, ("upper", "column"), 0, 0, tiled=True)

    return pl.pallas_call(
        final_kernel,
        grid=(4,),
        out_shape=jax.ShapeDtypeStruct((32, 64, LENGTH), jnp.float32),
        in_specs=[
            pl.BlockSpec((8, 64, LENGTH), lambda g: (g, 0, 0)),
            pl.BlockSpec((2, 1, 8, 32, LENGTH), lambda g: (0, g, 0, 0, 0)),
        ],
        out_specs=pl.BlockSpec((8, 64, LENGTH), lambda g: (g, 0, 0)),
        compiler_params=pltpu.CompilerParams(vmem_limit_bytes=16 << 20),
        name="final_kernel",
    )(estimate, logs.reshape(2, 4, 8, 32, LENGTH))


def solution(mesh):
    fine = Mesh(mesh.devices.reshape(2, 4, 32), ("upper", "column", "tile"))
    view = ("upper", "column")
    placed = (P("tile"), P(view, "tile"), P(view), P(view), P(view))
    return jax.shard_map(
        body, mesh=fine, in_specs=placed, out_specs=P("tile"), check_vma=False
    )
```

```python
import jax
import jax.numpy as jnp
from jax import lax
from jax.experimental import pallas as pl
from jax.experimental.pallas import tpu as pltpu
from jax.sharding import Mesh, PartitionSpec as P

PROFILE_SIGMA = 48.0
PAIR_SCALE = 32700.0 / 2.8
TOTAL_SCALE = PAIR_SCALE / 4.0
SLABS, ROWS, LENGTH = 32, 32, 256
TOTAL = SLABS * ROWS
GROUP = 4


def blur_matrix(profile):
    column = lax.broadcasted_iota(jnp.int32, (1, LENGTH), 1)
    distance = jnp.minimum(column, LENGTH - column).astype(jnp.float32)
    weights = profile * jnp.exp(-distance * distance / (2.0 * PROFILE_SIGMA * PROFILE_SIGMA))
    kernel = weights / jnp.sum(weights, axis=1, keepdims=True)
    rows = jnp.broadcast_to(kernel, (LENGTH, LENGTH))
    return pltpu.roll(rows, 0, 1, stride=1, stride_axis=0)


def tile_rows(wide, rest, turn, row):
    tiles = pltpu.roll(wide.reshape(-1, 8, LENGTH), turn, 1)
    count = tiles.shape[0]
    tiles = jnp.where(row < 8 - rest, tiles[: count - 1], tiles[1:])
    return tiles.reshape(8 * count - 8, LENGTH)


def blend_of(column, w):
    a = (w * 4 + column + 1).astype(jnp.float32) / 9.0
    return a, 1.0 - a


def pick_kernel(place_ref, est_ref, *refs):
    out_refs, (lines_ref, sem) = refs[:4], refs[4:]
    upper, column, tile = place_ref[0], place_ref[1], place_ref[2]
    tile_y, tile_z = lax.div(tile, 16), lax.rem(lax.div(tile, 2), 8)
    half = pl.ds(pl.multiple_of(32 * upper, 32), 32)
    copies = [
        pltpu.make_async_copy(
            est_ref.at[:, half, pl.ds(128 * h, 128)], lines_ref.at[h], sem.at[h]
        )
        for h in range(2)
    ]
    for copy in copies:
        copy.start()
    for copy in copies:
        copy.wait()
    rows_ref = lines_ref.reshape(2, ROWS * 32, 128)
    for k in range(4):
        y = lax.rem(tile_y + k // 2, 2)
        z = lax.rem(tile_z + column + 4 * (k % 2), 8)
        for c in range(2):
            for h in range(2):
                lanes = pl.ds(128 * h, 128)
                rows = rows_ref[h, pl.ds(16 * y + 2 * z + c, ROWS, stride=32)]
                out_refs[k][c, :, lanes] = rows.astype(jnp.bfloat16)


def forward_kernel(
    place_ref, own_ref, other_ref, own_profile_ref, other_profile_ref, est0_ref, est1_ref,
    est2_ref, est3_ref, inverse_ref, e_ref,
):
    est_refs = (est0_ref, est1_ref, est2_ref, est3_ref)
    upper, column, tile = place_ref[0], place_ref[1], place_ref[2]
    tile_y, tile_z, core = lax.div(tile, 16), lax.rem(lax.div(tile, 2), 8), lax.rem(tile, 2)

    for r, est_ref in enumerate(est_refs):
        source = lax.rem(column + 4 - r, 4)
        for k in range(4):
            y = lax.rem(tile_y + k // 2, 2)
            z = lax.rem(tile_z + 16 - source - 4 * (k % 2), 8)
            for c in range(2):
                slab = 16 * y + 2 * z + lax.rem(core + c, 2)
                base = pl.multiple_of(slab * ROWS + 8, 8)
                e_ref[pl.ds(base, ROWS)] = est_ref[c, k].astype(jnp.float32)
    e_ref[pl.ds(0, 8)] = e_ref[pl.ds(TOTAL, 8)]
    e_ref[pl.ds(TOTAL + 8, 16)] = e_ref[pl.ds(8, 16)]
    row = lax.broadcasted_iota(jnp.int32, (1, 8, LENGTH), 1)

    for w in range(2):
        is_own = upper == w
        shift = jnp.where(is_own, own_ref[0], other_ref[0])
        offset = jnp.where(is_own, own_ref[1], other_ref[1])
        a, b = blend_of(column, w)
        skip = lax.div(8 + offset, 8)
        rest = 8 + offset - 8 * skip
        turn = lax.rem(8 - rest, 8)
        profile = jnp.where(is_own, own_profile_ref[...], other_profile_ref[...])
        matrix = blur_matrix(profile).astype(jnp.bfloat16)

        def blur(k, c, w=w, a=a, b=b, matrix=matrix, skip=skip, rest=rest, turn=turn, shift=shift):
            base = pl.multiple_of(k * (ROWS * GROUP), ROWS * GROUP)
            parts = []
            for q in range(GROUP):
                s = lax.rem(k * GROUP + q + shift, SLABS)
                start = pl.multiple_of(s * ROWS + 8 * skip, 8)
                wide = tile_rows(e_ref[pl.ds(start, ROWS + 16)], rest, turn, row)
                parts.append(a * wide[:ROWS] + b * wide[1 : ROWS + 1])
            warped = jnp.concatenate(parts, axis=0).astype(jnp.bfloat16)
            forward = jnp.dot(warped, matrix, preferred_element_type=jnp.float32)
            inverse_ref[w, pl.ds(base, ROWS * GROUP)] = 1.0 / forward
            return c

        lax.fori_loop(0, SLABS // GROUP, blur, 0)


def back_kernel(
    place_ref, own_ref, other_ref, own_profile_ref, other_profile_ref, image_ref, inverse_ref,
    out_ref, b_ref,
):
    upper, column = place_ref[0], place_ref[1]
    row = lax.broadcasted_iota(jnp.int32, (1, 8, LENGTH), 1)

    for w in range(2):
        profile = jnp.where(upper == w, own_profile_ref[...], other_profile_ref[...])
        matrix = blur_matrix(profile).astype(jnp.bfloat16)

        def blur(k, c, w=w, matrix=matrix):
            base = pl.multiple_of(k * (ROWS * GROUP), ROWS * GROUP)
            image = image_ref[pl.ds(w * SLABS + k * GROUP, GROUP)].reshape(ROWS * GROUP, LENGTH)
            ratios = image.astype(jnp.float32) * inverse_ref[w, pl.ds(base, ROWS * GROUP)]
            b_ref[w, pl.ds(base + 16, ROWS * GROUP)] = lax.dot_general(
                ratios.astype(jnp.bfloat16),
                matrix,
                (((1,), (1,)), ((), ())),
                preferred_element_type=jnp.float32,
            )
            return c

        lax.fori_loop(0, SLABS // GROUP, blur, 0)
        b_ref[w, pl.ds(0, 16)] = b_ref[w, pl.ds(TOTAL, 16)]
        b_ref[w, pl.ds(TOTAL + 16, 8)] = b_ref[w, pl.ds(16, 8)]

    views = []
    for w in range(2):
        is_own = upper == w
        shift = jnp.where(is_own, own_ref[0], other_ref[0])
        offset = jnp.where(is_own, own_ref[1], other_ref[1])
        skip = lax.div(8 - offset, 8)
        rest = 8 - offset - 8 * skip
        views.append((shift, skip, rest, lax.rem(8 - rest, 8), *blend_of(column, w)))

    def join(s, c):
        product = None
        for w, (shift, skip, rest, turn, a, b) in enumerate(views):
            t = lax.rem(s - shift + SLABS, SLABS)
            start = pl.multiple_of(t * ROWS + 8 * skip, 8)
            wide = b_ref[w, pl.ds(start, ROWS + 16)]
            blended = a * wide[8:] + b * wide[7 : ROWS + 15]
            correction = tile_rows(blended, rest, turn, row)
            product = correction if product is None else product * correction
        code = jnp.clip(jnp.log(product) * PAIR_SCALE, -32767.0, 32767.0)
        code = jnp.floor(code + 0.5).astype(jnp.int32).astype(jnp.int16)
        for g in range(4):
            out_ref[g, s] = code[8 * g : 8 * g + 8]
        return c

    lax.fori_loop(0, SLABS, join, 0)


def final_kernel(est_ref, code_ref, out_ref):
    for h in range(2):
        lines = pl.ds(32 * h, 32)
        logs = code_ref[h, 0].astype(jnp.int32).astype(jnp.float32) * (1.0 / TOTAL_SCALE)
        out_ref[:, lines] = est_ref[:, lines] * jnp.exp(logs)


def distance_route(k):
    route = []
    for x in range(4):
        for y in range(2):
            for z in range(8):
                for c in range(2):
                    target = 16 * ((y + k // 2) % 2) + 2 * ((z + x + 4 * (k % 2)) % 8) + c
                    route.append((32 * x + 16 * y + 2 * z + c, 32 * x + target))
    return route


VMEM = pl.BlockSpec(memory_space=pltpu.VMEM)
SMEM = pl.BlockSpec(memory_space=pltpu.SMEM)


def body(estimate, measured, blur_profile, view_offset, tile_shift):
    upper = lax.axis_index("upper")
    column = lax.axis_index("column")
    swap = [(0, 1), (1, 0)]
    moves = jnp.concatenate([tile_shift, view_offset])
    other_moves = lax.ppermute(moves, "upper", swap)
    other_profile = lax.ppermute(blur_profile, "upper", swap)

    image = measured[0].transpose(1, 0, 2)
    image_lines = lax.all_to_all(image, ("upper", "tile"), 0, 0, tiled=True)
    tile = lax.axis_index("tile")
    place = jnp.stack([upper, column, tile])
    chips = pl.pallas_call(
        pick_kernel,
        out_shape=[jax.ShapeDtypeStruct((2, ROWS, LENGTH), jnp.bfloat16)] * 4,
        in_specs=[SMEM, pl.BlockSpec(memory_space=pl.ANY)],
        out_specs=[VMEM] * 4,
        scratch_shapes=[
            pltpu.VMEM((2, ROWS, 32, 128), jnp.float32),
            pltpu.SemaphoreType.DMA((2,)),
        ],
        cost_estimate=pl.CostEstimate(flops=0, bytes_accessed=2 << 20, transcendentals=0),
        compiler_params=pltpu.CompilerParams(vmem_limit_bytes=125 << 19),
        name="pick_kernel",
    )(place, estimate)
    arrived = [
        lax.ppermute(chip, ("column", "tile"), distance_route(k)) for k, chip in enumerate(chips)
    ]
    core = tile % 2
    arrived = jnp.stack(arrived, axis=1)
    mine = lax.dynamic_index_in_dim(arrived, core, 0, keepdims=False)
    given = lax.dynamic_index_in_dim(arrived, 1 - core, 0, keepdims=False)
    given = lax.ppermute(given, "tile", [(i, i ^ 1) for i in range(32)])
    piece = jnp.stack([mine, given])
    est_lines = [piece]
    for d in (1, 2, 3):
        route = [(i, (i + d) % 4) for i in range(4)]
        est_lines.append(lax.ppermute(piece, "column", route))

    inverse = pl.pallas_call(
        forward_kernel,
        out_shape=jax.ShapeDtypeStruct((2, TOTAL, LENGTH), jnp.float32),
        in_specs=[SMEM] * 3 + [VMEM] * 6,
        out_specs=VMEM,
        scratch_shapes=[pltpu.VMEM((TOTAL + 24, LENGTH), jnp.float32)],
        cost_estimate=pl.CostEstimate(
            flops=4 * TOTAL * LENGTH * LENGTH, bytes_accessed=8 << 20, transcendentals=0
        ),
        compiler_params=pltpu.CompilerParams(vmem_limit_bytes=16 << 20),
        name="forward_kernel",
    )(place, moves, other_moves, blur_profile, other_profile, *est_lines)
    codes = pl.pallas_call(
        back_kernel,
        out_shape=jax.ShapeDtypeStruct((4, SLABS, 8, LENGTH), jnp.int16),
        in_specs=[SMEM] * 3 + [VMEM] * 4,
        out_specs=VMEM,
        scratch_shapes=[pltpu.VMEM((2, TOTAL + 24, LENGTH), jnp.float32)],
        compiler_params=pltpu.CompilerParams(vmem_limit_bytes=16 << 20),
        name="back_kernel",
    )(place, moves, other_moves, blur_profile, other_profile, image_lines, inverse)
    codes = lax.all_to_all(codes, "column", 0, 0, tiled=True)
    total = jnp.sum(codes.astype(jnp.int32), axis=0)
    logs = ((total + 2) >> 2).astype(jnp.int16)
    logs = lax.all_to_all(logs, "tile", 0, 0, tiled=True)
    logs = jnp.broadcast_to(logs.transpose(1, 0, 2)[None], (8, 8, 32, LENGTH))
    logs = lax.all_to_all(logs, ("upper", "column"), 0, 0, tiled=True)

    return pl.pallas_call(
        final_kernel,
        grid=(4,),
        out_shape=jax.ShapeDtypeStruct((32, 64, LENGTH), jnp.float32),
        in_specs=[
            pl.BlockSpec((8, 64, LENGTH), lambda g: (g, 0, 0)),
            pl.BlockSpec((2, 1, 8, 32, LENGTH), lambda g: (0, g, 0, 0, 0)),
        ],
        out_specs=pl.BlockSpec((8, 64, LENGTH), lambda g: (g, 0, 0)),
        compiler_params=pltpu.CompilerParams(vmem_limit_bytes=16 << 20),
        name="final_kernel",
    )(estimate, logs.reshape(2, 4, 8, 32, LENGTH))


def solution(mesh):
    fine = Mesh(mesh.devices.reshape(2, 4, 32), ("upper", "column", "tile"))
    view = ("upper", "column")
    placed = (P("tile"), P(view, "tile"), P(view), P(view), P(view))
    return jax.shard_map(
        body, mesh=fine, in_specs=placed, out_specs=P("tile"), check_vma=False
    )
```

```python
import jax
import jax.numpy as jnp
from jax import lax
from jax.experimental import pallas as pl
from jax.experimental.pallas import tpu as pltpu
from jax.sharding import Mesh, PartitionSpec as P

PROFILE_SIGMA = 48.0
PAIR_SCALE = 32700.0 / 2.8
TOTAL_SCALE = PAIR_SCALE / 4.0
SLABS, ROWS, LENGTH = 32, 32, 256
TOTAL = SLABS * ROWS
GROUP = 4


def blur_matrix(profile):
    column = lax.broadcasted_iota(jnp.int32, (1, LENGTH), 1)
    distance = jnp.minimum(column, LENGTH - column).astype(jnp.float32)
    weights = profile * jnp.exp(-distance * distance / (2.0 * PROFILE_SIGMA * PROFILE_SIGMA))
    kernel = weights / jnp.sum(weights, axis=1, keepdims=True)
    rows = jnp.broadcast_to(kernel, (LENGTH, LENGTH))
    return pltpu.roll(rows, 0, 1, stride=1, stride_axis=0)


def tile_rows(wide, rest, turn, row):
    tiles = pltpu.roll(wide.reshape(-1, 8, LENGTH), turn, 1)
    count = tiles.shape[0]
    tiles = jnp.where(row < 8 - rest, tiles[: count - 1], tiles[1:])
    return tiles.reshape(8 * count - 8, LENGTH)


def blend_of(column, w):
    a = (w * 4 + column + 1).astype(jnp.float32) / 9.0
    return a, 1.0 - a


def pick_kernel(place_ref, est_ref, out0_ref, out1_ref, lines_ref, sem):
    upper, column, tile = place_ref[0], place_ref[1], place_ref[2]
    tile_y, tile_z = lax.div(tile, 16), lax.rem(lax.div(tile, 2), 8)
    z = lax.rem(tile_z + column + 4 * upper, 8)
    copies = []
    for k in range(2):
        for u in range(2):
            line = 32 * u + 16 * lax.rem(tile_y + k, 2) + 8 * lax.div(z, 4)
            for h in range(2):
                copy = pltpu.make_async_copy(
                    est_ref.at[:, pl.ds(pl.multiple_of(line, 8), 8), pl.ds(128 * h, 128)],
                    lines_ref.at[k, u, h],
                    sem.at[k, u, h],
                )
                copy.start()
                copies.append(copy)
    for copy in copies:
        copy.wait()
    rows_ref = lines_ref.reshape(2, 2, 2, ROWS * 8, 128)
    for k, out_ref in enumerate((out0_ref, out1_ref)):
        for u in range(2):
            for h in range(2):
                for c in range(2):
                    rows = rows_ref[k, u, h, pl.ds(2 * lax.rem(z, 4) + c, ROWS, stride=8)]
                    out_ref[u, c, :, pl.ds(128 * h, 128)] = rows.astype(jnp.bfloat16)


def forward_kernel(
    place_ref, own_ref, other_ref, own_profile_ref, other_profile_ref, est0_ref, est1_ref,
    est2_ref, est3_ref, inverse_ref, e_ref,
):
    est_refs = (est0_ref, est1_ref, est2_ref, est3_ref)
    upper, column, tile = place_ref[0], place_ref[1], place_ref[2]
    tile_y, tile_z, core = lax.div(tile, 16), lax.rem(lax.div(tile, 2), 8), lax.rem(tile, 2)

    for r, est_ref in enumerate(est_refs):
        source = lax.rem(column + 4 - r, 4)
        for u in range(2):
            z = lax.rem(tile_z + 16 - source - 4 * lax.rem(upper + u, 2), 8)
            for c in range(2):
                for k in range(2):
                    slab = 16 * lax.rem(tile_y + k, 2) + 2 * z + lax.rem(core + c, 2)
                    base = pl.multiple_of(slab * ROWS + 8, 8)
                    e_ref[pl.ds(base, ROWS)] = est_ref[u, c, k].astype(jnp.float32)
    e_ref[pl.ds(0, 8)] = e_ref[pl.ds(TOTAL, 8)]
    e_ref[pl.ds(TOTAL + 8, 16)] = e_ref[pl.ds(8, 16)]
    row = lax.broadcasted_iota(jnp.int32, (1, 8, LENGTH), 1)

    for w in range(2):
        is_own = upper == w
        shift = jnp.where(is_own, own_ref[0], other_ref[0])
        offset = jnp.where(is_own, own_ref[1], other_ref[1])
        a, b = blend_of(column, w)
        skip = lax.div(8 + offset, 8)
        rest = 8 + offset - 8 * skip
        turn = lax.rem(8 - rest, 8)
        profile = jnp.where(is_own, own_profile_ref[...], other_profile_ref[...])
        matrix = blur_matrix(profile).astype(jnp.bfloat16)

        def blur(k, c, w=w, a=a, b=b, matrix=matrix, skip=skip, rest=rest, turn=turn, shift=shift):
            base = pl.multiple_of(k * (ROWS * GROUP), ROWS * GROUP)
            parts = []
            for q in range(GROUP):
                s = lax.rem(k * GROUP + q + shift, SLABS)
                start = pl.multiple_of(s * ROWS + 8 * skip, 8)
                wide = tile_rows(e_ref[pl.ds(start, ROWS + 16)], rest, turn, row)
                parts.append(a * wide[:ROWS] + b * wide[1 : ROWS + 1])
            warped = jnp.concatenate(parts, axis=0).astype(jnp.bfloat16)
            forward = jnp.dot(warped, matrix, preferred_element_type=jnp.float32)
            inverse_ref[w, pl.ds(base, ROWS * GROUP)] = 1.0 / forward
            return c

        lax.fori_loop(0, SLABS // GROUP, blur, 0)


def back_kernel(
    place_ref, own_ref, other_ref, own_profile_ref, other_profile_ref, image_ref, inverse_ref,
    out_ref, b_ref,
):
    upper, column = place_ref[0], place_ref[1]
    row = lax.broadcasted_iota(jnp.int32, (1, 8, LENGTH), 1)

    for w in range(2):
        profile = jnp.where(upper == w, own_profile_ref[...], other_profile_ref[...])
        matrix = blur_matrix(profile).astype(jnp.bfloat16)

        def blur(k, c, w=w, matrix=matrix):
            base = pl.multiple_of(k * (ROWS * GROUP), ROWS * GROUP)
            image = image_ref[pl.ds(w * SLABS + k * GROUP, GROUP)].reshape(ROWS * GROUP, LENGTH)
            ratios = image.astype(jnp.float32) * inverse_ref[w, pl.ds(base, ROWS * GROUP)]
            b_ref[w, pl.ds(base + 16, ROWS * GROUP)] = lax.dot_general(
                ratios.astype(jnp.bfloat16),
                matrix,
                (((1,), (1,)), ((), ())),
                preferred_element_type=jnp.float32,
            )
            return c

        lax.fori_loop(0, SLABS // GROUP, blur, 0)
        b_ref[w, pl.ds(0, 16)] = b_ref[w, pl.ds(TOTAL, 16)]
        b_ref[w, pl.ds(TOTAL + 16, 8)] = b_ref[w, pl.ds(16, 8)]

    views = []
    for w in range(2):
        is_own = upper == w
        shift = jnp.where(is_own, own_ref[0], other_ref[0])
        offset = jnp.where(is_own, own_ref[1], other_ref[1])
        skip = lax.div(8 - offset, 8)
        rest = 8 - offset - 8 * skip
        views.append((shift, skip, rest, lax.rem(8 - rest, 8), *blend_of(column, w)))

    def join(s, c):
        product = None
        for w, (shift, skip, rest, turn, a, b) in enumerate(views):
            t = lax.rem(s - shift + SLABS, SLABS)
            start = pl.multiple_of(t * ROWS + 8 * skip, 8)
            wide = b_ref[w, pl.ds(start, ROWS + 16)]
            blended = a * wide[8:] + b * wide[7 : ROWS + 15]
            correction = tile_rows(blended, rest, turn, row)
            product = correction if product is None else product * correction
        code = jnp.clip(jnp.log(product) * PAIR_SCALE, -32767.0, 32767.0)
        code = jnp.floor(code + 0.5).astype(jnp.int32).astype(jnp.int16)
        for g in range(4):
            out_ref[g, s] = code[8 * g : 8 * g + 8]
        return c

    lax.fori_loop(0, SLABS, join, 0)


def final_kernel(est_ref, code_ref, out_ref):
    for h in range(2):
        lines = pl.ds(32 * h, 32)
        logs = code_ref[h, 0].astype(jnp.int32).astype(jnp.float32) * (1.0 / TOTAL_SCALE)
        out_ref[:, lines] = est_ref[:, lines] * jnp.exp(logs)


def distance_route(k):
    route = []
    for v in range(8):
        for y in range(2):
            for z in range(8):
                for c in range(2):
                    target = 16 * ((y + k) % 2) + 2 * ((z + v) % 8) + c
                    route.append((32 * v + 16 * y + 2 * z + c, 32 * v + target))
    return route


VMEM = pl.BlockSpec(memory_space=pltpu.VMEM)
SMEM = pl.BlockSpec(memory_space=pltpu.SMEM)


def update(estimate, measured, blur_profile, view_offset, tile_shift):
    upper = lax.axis_index("upper")
    column = lax.axis_index("column")
    swap = [(0, 1), (1, 0)]
    moves = jnp.concatenate([tile_shift, view_offset])
    other_moves = lax.ppermute(moves, "upper", swap)
    other_profile = lax.ppermute(blur_profile, "upper", swap)

    tile = lax.axis_index("tile")
    core = tile % 2
    place = jnp.stack([upper, column, tile])
    chips = pl.pallas_call(
        pick_kernel,
        out_shape=[jax.ShapeDtypeStruct((2, 2, ROWS, LENGTH), jnp.bfloat16)] * 2,
        in_specs=[SMEM, pl.BlockSpec(memory_space=pl.ANY)],
        out_specs=[VMEM] * 2,
        scratch_shapes=[
            pltpu.VMEM((2, 2, 2, ROWS, 8, 128), jnp.float32),
            pltpu.SemaphoreType.DMA((2, 2, 2)),
        ],
        cost_estimate=pl.CostEstimate(flops=0, bytes_accessed=2 << 20, transcendentals=0),
        compiler_params=pltpu.CompilerParams(vmem_limit_bytes=125 << 19),
        name="pick_kernel",
    )(place, estimate)
    arrived = []
    for k, chip in enumerate(chips):
        arrived.append(lax.ppermute(chip, ("upper", "column", "tile"), distance_route(k)))
    image = measured[0].transpose(1, 0, 2)
    image_lines = lax.all_to_all(image, ("upper", "tile"), 0, 0, tiled=True)

    arrived = jnp.stack(arrived, axis=0)
    mine = lax.dynamic_index_in_dim(arrived, core, 2, keepdims=False)
    given = lax.dynamic_index_in_dim(arrived, 1 - core, 2, keepdims=False)
    given = lax.ppermute(given, "tile", [(i, i ^ 1) for i in range(32)])
    both = jnp.stack([mine, given])
    mine = lax.dynamic_index_in_dim(both, upper, 2, keepdims=False)
    given = lax.dynamic_index_in_dim(both, 1 - upper, 2, keepdims=False)
    given = lax.ppermute(given, "upper", swap)
    piece = jnp.stack([mine, given])
    est_lines = [piece]
    for d in (1, 2, 3):
        route = [(i, (i + d) % 4) for i in range(4)]
        est_lines.append(lax.ppermute(piece, "column", route))

    inverse = pl.pallas_call(
        forward_kernel,
        out_shape=jax.ShapeDtypeStruct((2, TOTAL, LENGTH), jnp.float32),
        in_specs=[SMEM] * 3 + [VMEM] * 6,
        out_specs=VMEM,
        scratch_shapes=[pltpu.VMEM((TOTAL + 24, LENGTH), jnp.float32)],
        cost_estimate=pl.CostEstimate(
            flops=4 * TOTAL * LENGTH * LENGTH, bytes_accessed=8 << 20, transcendentals=0
        ),
        compiler_params=pltpu.CompilerParams(vmem_limit_bytes=16 << 20),
        name="forward_kernel",
    )(place, moves, other_moves, blur_profile, other_profile, *est_lines)
    codes = pl.pallas_call(
        back_kernel,
        out_shape=jax.ShapeDtypeStruct((4, SLABS, 8, LENGTH), jnp.int16),
        in_specs=[SMEM] * 3 + [VMEM] * 4,
        out_specs=VMEM,
        scratch_shapes=[pltpu.VMEM((2, TOTAL + 24, LENGTH), jnp.float32)],
        compiler_params=pltpu.CompilerParams(vmem_limit_bytes=16 << 20),
        name="back_kernel",
    )(place, moves, other_moves, blur_profile, other_profile, image_lines, inverse)
    codes = lax.all_to_all(codes, "column", 0, 0, tiled=True)
    total = jnp.sum(codes.astype(jnp.int32), axis=0)
    logs = ((total + 2) >> 2).astype(jnp.int16)
    logs = lax.all_to_all(logs, "tile", 0, 0, tiled=True)
    logs = jnp.broadcast_to(logs.transpose(1, 0, 2)[None], (8, 8, 32, LENGTH))
    logs = lax.all_to_all(logs, ("upper", "column"), 0, 0, tiled=True)

    return pl.pallas_call(
        final_kernel,
        grid=(4,),
        out_shape=jax.ShapeDtypeStruct((32, 64, LENGTH), jnp.float32),
        in_specs=[
            pl.BlockSpec((8, 64, LENGTH), lambda g: (g, 0, 0)),
            pl.BlockSpec((2, 1, 8, 32, LENGTH), lambda g: (0, g, 0, 0, 0)),
        ],
        out_specs=pl.BlockSpec((8, 64, LENGTH), lambda g: (g, 0, 0)),
        compiler_params=pltpu.CompilerParams(vmem_limit_bytes=16 << 20),
        name="final_kernel",
    )(estimate, logs.reshape(2, 4, 8, 32, LENGTH))


def solution(mesh):
    fine = Mesh(mesh.devices.reshape(2, 4, 32), ("upper", "column", "tile"))
    view = ("upper", "column")
    placed = (P("tile"), P(view, "tile"), P(view), P(view), P(view))
    return jax.shard_map(update, mesh=fine, in_specs=placed, out_specs=P("tile"), check_vma=False)
```

```python
import jax
import jax.numpy as jnp
from jax import lax
from jax.experimental import pallas as pl
from jax.experimental.pallas import tpu as pltpu
from jax.sharding import Mesh, PartitionSpec as P

PROFILE_SIGMA = 48.0
PAIR_SCALE = 32700.0 / 2.8
TOTAL_SCALE = PAIR_SCALE / 4.0
SLABS, ROWS, LENGTH = 32, 32, 256
TOTAL = SLABS * ROWS
GROUP = 4


def blur_matrix(profile):
    column = lax.broadcasted_iota(jnp.int32, (1, LENGTH), 1)
    distance = jnp.minimum(column, LENGTH - column).astype(jnp.float32)
    weights = profile * jnp.exp(-distance * distance / (2.0 * PROFILE_SIGMA * PROFILE_SIGMA))
    kernel = weights / jnp.sum(weights, axis=1, keepdims=True)
    rows = jnp.broadcast_to(kernel, (LENGTH, LENGTH))
    return pltpu.roll(rows, 0, 1, stride=1, stride_axis=0)


def tile_rows(wide, rest, turn, row):
    tiles = pltpu.roll(wide.reshape(-1, 8, LENGTH), turn, 1)
    count = tiles.shape[0]
    tiles = jnp.where(row < 8 - rest, tiles[: count - 1], tiles[1:])
    return tiles.reshape(8 * count - 8, LENGTH)


def blend_of(column, w):
    a = (w * 4 + column + 1).astype(jnp.float32) / 9.0
    return a, 1.0 - a


def place():
    tile = lax.axis_index("tile")
    return lax.axis_index("upper"), lax.axis_index("column"), tile


def pick_kernel(est_ref, out0_ref, out1_ref, lines_ref, sem):
    upper, column, tile = place()
    tile_y, tile_z = lax.div(tile, 16), lax.rem(lax.div(tile, 2), 8)
    z = lax.rem(tile_z + column + 4 * upper, 8)
    copies = []
    for k in range(2):
        for u in range(2):
            line = 32 * u + 16 * lax.rem(tile_y + k, 2) + 8 * lax.div(z, 4)
            for h in range(2):
                copy = pltpu.make_async_copy(
                    est_ref.at[:, pl.ds(pl.multiple_of(line, 8), 8), pl.ds(128 * h, 128)],
                    lines_ref.at[k, u, h],
                    sem.at[k, u, h],
                )
                copy.start()
                copies.append(copy)
    for copy in copies:
        copy.wait()
    rows_ref = lines_ref.reshape(2, 2, 2, ROWS * 8, 128)
    for k, out_ref in enumerate((out0_ref, out1_ref)):
        for u in range(2):
            for h in range(2):
                for c in range(2):
                    rows = rows_ref[k, u, h, pl.ds(2 * lax.rem(z, 4) + c, ROWS, stride=8)]
                    out_ref[u, c, :, pl.ds(128 * h, 128)] = rows.astype(jnp.bfloat16)


def forward_kernel(
    shift_ref, offset_ref, other_ref, own_profile_ref, other_profile_ref, est0_ref, est1_ref,
    est2_ref, est3_ref, inverse_ref, e_ref,
):
    est_refs = (est0_ref, est1_ref, est2_ref, est3_ref)
    upper, column, tile = place()
    tile_y, tile_z, core = lax.div(tile, 16), lax.rem(lax.div(tile, 2), 8), lax.rem(tile, 2)

    for r, est_ref in enumerate(est_refs):
        source = lax.rem(column + 4 - r, 4)
        for u in range(2):
            z = lax.rem(tile_z + 16 - source - 4 * lax.rem(upper + u, 2), 8)
            for c in range(2):
                for k in range(2):
                    slab = 16 * lax.rem(tile_y + k, 2) + 2 * z + lax.rem(core + c, 2)
                    base = pl.multiple_of(slab * ROWS + 8, 8)
                    e_ref[pl.ds(base, ROWS)] = est_ref[u, c, k].astype(jnp.float32)
    e_ref[pl.ds(0, 8)] = e_ref[pl.ds(TOTAL, 8)]
    e_ref[pl.ds(TOTAL + 8, 16)] = e_ref[pl.ds(8, 16)]
    row = lax.broadcasted_iota(jnp.int32, (1, 8, LENGTH), 1)

    for w in range(2):
        is_own = upper == w
        shift = jnp.where(is_own, shift_ref[0], other_ref[0, LENGTH].astype(jnp.int32))
        offset = jnp.where(is_own, offset_ref[0], other_ref[0, LENGTH + 1].astype(jnp.int32))
        a, b = blend_of(column, w)
        skip = lax.div(8 + offset, 8)
        rest = 8 + offset - 8 * skip
        turn = lax.rem(8 - rest, 8)
        profile = jnp.where(is_own, own_profile_ref[...], other_profile_ref[:, pl.ds(0, LENGTH)])
        matrix = blur_matrix(profile).astype(jnp.bfloat16)

        def blur(k, c, w=w, a=a, b=b, matrix=matrix, skip=skip, rest=rest, turn=turn, shift=shift):
            base = pl.multiple_of(k * (ROWS * GROUP), ROWS * GROUP)
            parts = []
            for q in range(GROUP):
                s = lax.rem(k * GROUP + q + shift, SLABS)
                start = pl.multiple_of(s * ROWS + 8 * skip, 8)
                wide = tile_rows(e_ref[pl.ds(start, ROWS + 16)], rest, turn, row)
                parts.append(a * wide[:ROWS] + b * wide[1 : ROWS + 1])
            warped = jnp.concatenate(parts, axis=0).astype(jnp.bfloat16)
            forward = jnp.dot(warped, matrix, preferred_element_type=jnp.float32)
            inverse_ref[w, pl.ds(base, ROWS * GROUP)] = 1.0 / forward
            return c

        lax.fori_loop(0, SLABS // GROUP, blur, 0)


def back_kernel(
    shift_ref, offset_ref, other_ref, own_profile_ref, other_profile_ref, image_ref, inverse_ref,
    out_ref, b_ref,
):
    upper, column, _ = place()
    row = lax.broadcasted_iota(jnp.int32, (1, 8, LENGTH), 1)

    for w in range(2):
        profile = jnp.where(upper == w, own_profile_ref[...], other_profile_ref[:, pl.ds(0, LENGTH)])
        matrix = blur_matrix(profile).astype(jnp.bfloat16)

        def blur(k, c, w=w, matrix=matrix):
            base = pl.multiple_of(k * (ROWS * GROUP), ROWS * GROUP)
            image = image_ref[pl.ds(w * SLABS + k * GROUP, GROUP)].reshape(ROWS * GROUP, LENGTH)
            ratios = image.astype(jnp.float32) * inverse_ref[w, pl.ds(base, ROWS * GROUP)]
            b_ref[w, pl.ds(base + 16, ROWS * GROUP)] = lax.dot_general(
                ratios.astype(jnp.bfloat16),
                matrix,
                (((1,), (1,)), ((), ())),
                preferred_element_type=jnp.float32,
            )
            return c

        lax.fori_loop(0, SLABS // GROUP, blur, 0)
        b_ref[w, pl.ds(0, 16)] = b_ref[w, pl.ds(TOTAL, 16)]
        b_ref[w, pl.ds(TOTAL + 16, 8)] = b_ref[w, pl.ds(16, 8)]

    views = []
    for w in range(2):
        is_own = upper == w
        shift = jnp.where(is_own, shift_ref[0], other_ref[0, LENGTH].astype(jnp.int32))
        offset = jnp.where(is_own, offset_ref[0], other_ref[0, LENGTH + 1].astype(jnp.int32))
        skip = lax.div(8 - offset, 8)
        rest = 8 - offset - 8 * skip
        views.append((shift, skip, rest, lax.rem(8 - rest, 8), *blend_of(column, w)))

    def join(s, c):
        product = None
        for w, (shift, skip, rest, turn, a, b) in enumerate(views):
            t = lax.rem(s - shift + SLABS, SLABS)
            start = pl.multiple_of(t * ROWS + 8 * skip, 8)
            wide = b_ref[w, pl.ds(start, ROWS + 16)]
            blended = a * wide[8:] + b * wide[7 : ROWS + 15]
            correction = tile_rows(blended, rest, turn, row)
            product = correction if product is None else product * correction
        code = jnp.clip(jnp.log(product) * PAIR_SCALE, -32767.0, 32767.0)
        code = jnp.floor(code + 0.5).astype(jnp.int32).astype(jnp.int16)
        for g in range(4):
            out_ref[lax.rem(g - column + 4, 4), s] = code[8 * g : 8 * g + 8]
        return c

    lax.fori_loop(0, SLABS, join, 0)


def final_kernel(est_ref, code_ref, out_ref):
    for h in range(2):
        lines = pl.ds(32 * h, 32)
        logs = code_ref[h, 0].astype(jnp.int32).astype(jnp.float32) * (1.0 / TOTAL_SCALE)
        out_ref[:, lines] = est_ref[:, lines] * jnp.exp(logs)


def distance_route(k):
    route = []
    for v in range(8):
        for y in range(2):
            for z in range(8):
                for c in range(2):
                    target = 16 * ((y + k) % 2) + 2 * ((z + v) % 8) + c
                    route.append((32 * v + 16 * y + 2 * z + c, 32 * v + target))
    return route


VMEM = pl.BlockSpec(memory_space=pltpu.VMEM)
SMEM = pl.BlockSpec(memory_space=pltpu.SMEM)


def update(estimate, measured, blur_profile, view_offset, tile_shift):
    upper = lax.axis_index("upper")
    swap = [(0, 1), (1, 0)]
    moves = jnp.concatenate([tile_shift, view_offset]).astype(jnp.float32)
    info = jnp.concatenate([blur_profile, jnp.pad(moves, (0, 126))[None]], axis=1)
    other = lax.ppermute(info, "upper", swap)

    tile = lax.axis_index("tile")
    core = tile % 2
    chips = pl.pallas_call(
        pick_kernel,
        out_shape=[jax.ShapeDtypeStruct((2, 2, ROWS, LENGTH), jnp.bfloat16)] * 2,
        in_specs=[pl.BlockSpec(memory_space=pl.ANY)],
        out_specs=[VMEM] * 2,
        scratch_shapes=[
            pltpu.VMEM((2, 2, 2, ROWS, 8, 128), jnp.float32),
            pltpu.SemaphoreType.DMA((2, 2, 2)),
        ],
        cost_estimate=pl.CostEstimate(flops=0, bytes_accessed=2 << 20, transcendentals=0),
        compiler_params=pltpu.CompilerParams(vmem_limit_bytes=125 << 19),
        name="pick_kernel",
    )(estimate)
    arrived = []
    for k, chip in enumerate(chips):
        arrived.append(lax.ppermute(chip, ("upper", "column", "tile"), distance_route(k)))
    image = measured[0].transpose(1, 0, 2)
    image_lines = lax.all_to_all(image, ("upper", "tile"), 0, 0, tiled=True)

    arrived = jnp.stack(arrived, axis=0)
    mine = lax.dynamic_index_in_dim(arrived, core, 2, keepdims=False)
    given = lax.dynamic_index_in_dim(arrived, 1 - core, 2, keepdims=False)
    given = lax.ppermute(given, "tile", [(i, i ^ 1) for i in range(32)])
    both = jnp.stack([mine, given])
    mine = lax.dynamic_index_in_dim(both, upper, 2, keepdims=False)
    given = lax.dynamic_index_in_dim(both, 1 - upper, 2, keepdims=False)
    given = lax.ppermute(given, "upper", swap)
    piece = jnp.stack([mine, given])
    est_lines = [piece]
    for d in (1, 2, 3):
        route = [(i, (i + d) % 4) for i in range(4)]
        est_lines.append(lax.ppermute(piece, "column", route))

    inverse = pl.pallas_call(
        forward_kernel,
        out_shape=jax.ShapeDtypeStruct((2, TOTAL, LENGTH), jnp.float32),
        in_specs=[SMEM] * 3 + [VMEM] * 6,
        out_specs=VMEM,
        scratch_shapes=[pltpu.VMEM((TOTAL + 24, LENGTH), jnp.float32)],
        cost_estimate=pl.CostEstimate(
            flops=4 * TOTAL * LENGTH * LENGTH, bytes_accessed=8 << 20, transcendentals=0
        ),
        compiler_params=pltpu.CompilerParams(vmem_limit_bytes=16 << 20),
        name="forward_kernel",
    )(tile_shift, view_offset, other, blur_profile, other, *est_lines)
    codes = pl.pallas_call(
        back_kernel,
        out_shape=jax.ShapeDtypeStruct((4, SLABS, 8, LENGTH), jnp.int16),
        in_specs=[SMEM] * 3 + [VMEM] * 4,
        out_specs=VMEM,
        scratch_shapes=[pltpu.VMEM((2, TOTAL + 24, LENGTH), jnp.float32)],
        compiler_params=pltpu.CompilerParams(vmem_limit_bytes=16 << 20),
        name="back_kernel",
    )(tile_shift, view_offset, other, blur_profile, other, image_lines, inverse)
    total = codes[0].astype(jnp.int32)
    for d in (2, 1, 3):
        route = [(i, (i + d) % 4) for i in range(4)]
        total += lax.ppermute(codes[d], "column", route).astype(jnp.int32)
    logs = ((total + 2) >> 2).astype(jnp.int16)
    logs = lax.all_to_all(logs, "tile", 0, 0, tiled=True)
    logs = jnp.broadcast_to(logs.transpose(1, 0, 2)[None], (8, 8, 32, LENGTH))
    logs = lax.all_to_all(logs, ("upper", "column"), 0, 0, tiled=True)

    return pl.pallas_call(
        final_kernel,
        grid=(4,),
        out_shape=jax.ShapeDtypeStruct((32, 64, LENGTH), jnp.float32),
        in_specs=[
            pl.BlockSpec((8, 64, LENGTH), lambda g: (g, 0, 0)),
            pl.BlockSpec((2, 1, 8, 32, LENGTH), lambda g: (0, g, 0, 0, 0)),
        ],
        out_specs=pl.BlockSpec((8, 64, LENGTH), lambda g: (g, 0, 0)),
        compiler_params=pltpu.CompilerParams(vmem_limit_bytes=16 << 20),
        name="final_kernel",
    )(estimate, logs.reshape(2, 4, 8, 32, LENGTH))


def solution(mesh):
    fine = Mesh(mesh.devices.reshape(2, 4, 32), ("upper", "column", "tile"))
    view = ("upper", "column")
    placed = (P("tile"), P(view, "tile"), P(view), P(view), P(view))
    return jax.shard_map(update, mesh=fine, in_specs=placed, out_specs=P("tile"), check_vma=False)
```

```python
import jax
import jax.numpy as jnp
from jax import lax
from jax.experimental import pallas as pl
from jax.experimental.pallas import tpu as pltpu
from jax.sharding import Mesh, PartitionSpec as P

PROFILE_SIGMA = 48.0
PAIR_SCALE = 32700.0 / 2.8
TOTAL_SCALE = PAIR_SCALE / 4.0
SLABS, ROWS, LENGTH = 32, 32, 256
TOTAL = SLABS * ROWS
GROUP = 4


def blur_matrix(profile):
    column = lax.broadcasted_iota(jnp.int32, (1, LENGTH), 1)
    distance = jnp.minimum(column, LENGTH - column).astype(jnp.float32)
    weights = profile * jnp.exp(-distance * distance / (2.0 * PROFILE_SIGMA * PROFILE_SIGMA))
    kernel = weights / jnp.sum(weights, axis=1, keepdims=True)
    rows = jnp.broadcast_to(kernel, (LENGTH, LENGTH))
    return pltpu.roll(rows, 0, 1, stride=1, stride_axis=0)


def tile_rows(wide, rest, turn, row):
    tiles = pltpu.roll(wide.reshape(-1, 8, LENGTH), turn, 1)
    count = tiles.shape[0]
    tiles = jnp.where(row < 8 - rest, tiles[: count - 1], tiles[1:])
    return tiles.reshape(8 * count - 8, LENGTH)


def blend_of(column, w):
    a = (w * 4 + column + 1).astype(jnp.float32) / 9.0
    return a, 1.0 - a


def place():
    tile = lax.axis_index("tile")
    return lax.axis_index("upper"), lax.axis_index("column"), tile


def pick_kernel(est_ref, out_ref, lines_ref, sem):
    upper, column, tile = place()
    tile_y, tile_z = lax.div(tile, 16), lax.rem(lax.div(tile, 2), 8)
    z = lax.rem(tile_z + column + 4 * upper, 8)
    copies = []
    for k in range(2):
        for u in range(2):
            line = 32 * u + 16 * lax.rem(tile_y + k, 2) + 8 * lax.div(z, 4)
            for h in range(2):
                copy = pltpu.make_async_copy(
                    est_ref.at[:, pl.ds(pl.multiple_of(line, 8), 8), pl.ds(128 * h, 128)],
                    lines_ref.at[k, u, h],
                    sem.at[k, u, h],
                )
                copy.start()
                copies.append(copy)
    rows_ref = lines_ref.reshape(2, 2, 2, ROWS * 8, 128)
    for k in range(2):
        for u in range(2):
            for h in range(2):
                copies[4 * k + 2 * u + h].wait()
                for c in range(2):
                    rows = rows_ref[k, u, h, pl.ds(2 * lax.rem(z, 4) + c, ROWS, stride=8)]
                    out_ref[c, k, u, :, pl.ds(128 * h, 128)] = rows.astype(jnp.bfloat16)


def forward_kernel(
    shift_ref, offset_ref, other_ref, own_profile_ref, other_profile_ref, est0_ref, est1_ref,
    est2_ref, est3_ref, inverse_ref, e_ref,
):
    est_refs = (est0_ref, est1_ref, est2_ref, est3_ref)
    upper, column, tile = place()
    tile_y, tile_z, core = lax.div(tile, 16), lax.rem(lax.div(tile, 2), 8), lax.rem(tile, 2)

    for r, est_ref in enumerate(est_refs):
        source = lax.rem(column + 4 - r, 4)
        for u in range(2):
            z = lax.rem(tile_z + 16 - source - 4 * lax.rem(upper + u, 2), 8)
            for c in range(2):
                for k in range(2):
                    slab = 16 * lax.rem(tile_y + k, 2) + 2 * z + lax.rem(core + c, 2)
                    base = pl.multiple_of(slab * ROWS + 8, 8)
                    e_ref[pl.ds(base, ROWS)] = est_ref[u, k, c].astype(jnp.float32)
    e_ref[pl.ds(0, 8)] = e_ref[pl.ds(TOTAL, 8)]
    e_ref[pl.ds(TOTAL + 8, 16)] = e_ref[pl.ds(8, 16)]
    row = lax.broadcasted_iota(jnp.int32, (1, 8, LENGTH), 1)

    for w in range(2):
        is_own = upper == w
        shift = jnp.where(is_own, shift_ref[0], other_ref[0, LENGTH].astype(jnp.int32))
        offset = jnp.where(is_own, offset_ref[0], other_ref[0, LENGTH + 1].astype(jnp.int32))
        a, b = blend_of(column, w)
        skip = lax.div(8 + offset, 8)
        rest = 8 + offset - 8 * skip
        turn = lax.rem(8 - rest, 8)
        profile = jnp.where(is_own, own_profile_ref[...], other_profile_ref[:, pl.ds(0, LENGTH)])
        matrix = blur_matrix(profile).astype(jnp.bfloat16)

        def blur(k, c, w=w, a=a, b=b, matrix=matrix, skip=skip, rest=rest, turn=turn, shift=shift):
            base = pl.multiple_of(k * (ROWS * GROUP), ROWS * GROUP)
            parts = []
            for q in range(GROUP):
                s = lax.rem(k * GROUP + q + shift, SLABS)
                start = pl.multiple_of(s * ROWS + 8 * skip, 8)
                wide = tile_rows(e_ref[pl.ds(start, ROWS + 16)], rest, turn, row)
                parts.append(a * wide[:ROWS] + b * wide[1 : ROWS + 1])
            warped = jnp.concatenate(parts, axis=0).astype(jnp.bfloat16)
            forward = jnp.dot(warped, matrix, preferred_element_type=jnp.float32)
            inverse_ref[w, pl.ds(base, ROWS * GROUP)] = 1.0 / forward
            return c

        lax.fori_loop(0, SLABS // GROUP, blur, 0)


def back_kernel(
    shift_ref, offset_ref, other_ref, own_profile_ref, other_profile_ref, image_ref, inverse_ref,
    out_ref, b_ref,
):
    upper, column, _ = place()
    row = lax.broadcasted_iota(jnp.int32, (1, 8, LENGTH), 1)

    for w in range(2):
        profile = jnp.where(upper == w, own_profile_ref[...], other_profile_ref[:, pl.ds(0, LENGTH)])
        matrix = blur_matrix(profile).astype(jnp.bfloat16)

        def blur(k, c, w=w, matrix=matrix):
            base = pl.multiple_of(k * (ROWS * GROUP), ROWS * GROUP)
            image = image_ref[pl.ds(w * SLABS + k * GROUP, GROUP)].reshape(ROWS * GROUP, LENGTH)
            ratios = image.astype(jnp.float32) * inverse_ref[w, pl.ds(base, ROWS * GROUP)]
            b_ref[w, pl.ds(base + 16, ROWS * GROUP)] = lax.dot_general(
                ratios.astype(jnp.bfloat16),
                matrix,
                (((1,), (1,)), ((), ())),
                preferred_element_type=jnp.float32,
            )
            return c

        lax.fori_loop(0, SLABS // GROUP, blur, 0)
        b_ref[w, pl.ds(0, 16)] = b_ref[w, pl.ds(TOTAL, 16)]
        b_ref[w, pl.ds(TOTAL + 16, 8)] = b_ref[w, pl.ds(16, 8)]

    views = []
    for w in range(2):
        is_own = upper == w
        shift = jnp.where(is_own, shift_ref[0], other_ref[0, LENGTH].astype(jnp.int32))
        offset = jnp.where(is_own, offset_ref[0], other_ref[0, LENGTH + 1].astype(jnp.int32))
        skip = lax.div(8 - offset, 8)
        rest = 8 - offset - 8 * skip
        views.append((shift, skip, rest, lax.rem(8 - rest, 8), *blend_of(column, w)))

    def join(s, c):
        product = None
        for w, (shift, skip, rest, turn, a, b) in enumerate(views):
            t = lax.rem(s - shift + SLABS, SLABS)
            start = pl.multiple_of(t * ROWS + 8 * skip, 8)
            wide = b_ref[w, pl.ds(start, ROWS + 16)]
            blended = a * wide[8:] + b * wide[7 : ROWS + 15]
            correction = tile_rows(blended, rest, turn, row)
            product = correction if product is None else product * correction
        code = jnp.clip(jnp.log(product) * PAIR_SCALE, -32767.0, 32767.0)
        code = jnp.floor(code + 0.5).astype(jnp.int32).astype(jnp.int16)
        for g in range(4):
            out_ref[lax.rem(g - column + 4, 4), s] = code[8 * g : 8 * g + 8]
        return c

    lax.fori_loop(0, SLABS, join, 0)


def final_kernel(est_ref, code_ref, out_ref):
    for h in range(2):
        lines = pl.ds(32 * h, 32)
        logs = code_ref[h, 0].astype(jnp.int32).astype(jnp.float32) * (1.0 / TOTAL_SCALE)
        out_ref[:, lines] = est_ref[:, lines] * jnp.exp(logs)


def distance_route():
    route = []
    for v in range(8):
        for y in range(2):
            for z in range(8):
                for c in range(2):
                    target = 16 * y + 2 * ((z + v) % 8) + c
                    route.append((32 * v + 16 * y + 2 * z + c, 32 * v + target))
    return route


def swap_halves(block, axis, route, keep):
    mine = lax.dynamic_index_in_dim(block, keep, 0, keepdims=False)
    given = lax.dynamic_index_in_dim(block, 1 - keep, 0, keepdims=False)
    return mine, lax.ppermute(given, axis, route)


VMEM = pl.BlockSpec(memory_space=pltpu.VMEM)
SMEM = pl.BlockSpec(memory_space=pltpu.SMEM)


def update(estimate, measured, blur_profile, view_offset, tile_shift):
    upper = lax.axis_index("upper")
    swap = [(0, 1), (1, 0)]
    moves = jnp.concatenate([tile_shift, view_offset]).astype(jnp.float32)
    info = jnp.concatenate([blur_profile, jnp.pad(moves, (0, 126))[None]], axis=1)
    other = lax.ppermute(info, "upper", swap)

    tile = lax.axis_index("tile")
    chip = pl.pallas_call(
        pick_kernel,
        out_shape=jax.ShapeDtypeStruct((2, 2, 2, ROWS, LENGTH), jnp.bfloat16),
        in_specs=[pl.BlockSpec(memory_space=pl.ANY)],
        out_specs=VMEM,
        scratch_shapes=[
            pltpu.VMEM((2, 2, 2, ROWS, 8, 128), jnp.float32),
            pltpu.SemaphoreType.DMA((2, 2, 2)),
        ],
        cost_estimate=pl.CostEstimate(flops=0, bytes_accessed=2 << 20, transcendentals=0),
        compiler_params=pltpu.CompilerParams(vmem_limit_bytes=125 << 19),
        name="pick_kernel",
    )(estimate)
    block = lax.ppermute(chip, ("upper", "column", "tile"), distance_route())
    image = measured[0].transpose(1, 0, 2)
    image_lines = lax.all_to_all(image, ("upper", "tile"), 0, 0, tiled=True)

    pair = swap_halves(block, "tile", [(i, i ^ 1) for i in range(32)], tile % 2)
    block = jnp.stack(pair, axis=2)
    mine, given = block[0], block[1]
    given = lax.ppermute(given, "tile", [(i, i ^ 16) for i in range(32)])
    block = jnp.stack([mine, given], axis=1)
    pair = swap_halves(block, "upper", swap, upper)
    piece = jnp.stack(pair)
    est_lines = [piece]
    for d in (1, 2, 3):
        route = [(i, (i + d) % 4) for i in range(4)]
        est_lines.append(lax.ppermute(piece, "column", route))

    inverse = pl.pallas_call(
        forward_kernel,
        out_shape=jax.ShapeDtypeStruct((2, TOTAL, LENGTH), jnp.float32),
        in_specs=[SMEM] * 3 + [VMEM] * 6,
        out_specs=VMEM,
        scratch_shapes=[pltpu.VMEM((TOTAL + 24, LENGTH), jnp.float32)],
        cost_estimate=pl.CostEstimate(
            flops=4 * TOTAL * LENGTH * LENGTH, bytes_accessed=8 << 20, transcendentals=0
        ),
        compiler_params=pltpu.CompilerParams(vmem_limit_bytes=16 << 20),
        name="forward_kernel",
    )(tile_shift, view_offset, other, blur_profile, other, *est_lines)
    codes = pl.pallas_call(
        back_kernel,
        out_shape=jax.ShapeDtypeStruct((4, SLABS, 8, LENGTH), jnp.int16),
        in_specs=[SMEM] * 3 + [VMEM] * 4,
        out_specs=VMEM,
        scratch_shapes=[pltpu.VMEM((2, TOTAL + 24, LENGTH), jnp.float32)],
        compiler_params=pltpu.CompilerParams(vmem_limit_bytes=16 << 20),
        name="back_kernel",
    )(tile_shift, view_offset, other, blur_profile, other, image_lines, inverse)
    total = codes[0].astype(jnp.int32)
    for d in (2, 1, 3):
        route = [(i, (i + d) % 4) for i in range(4)]
        total += lax.ppermute(codes[d], "column", route).astype(jnp.int32)
    logs = ((total + 2) >> 2).astype(jnp.int16)
    logs = lax.all_to_all(logs, "tile", 0, 0, tiled=True)
    logs = jnp.broadcast_to(logs.transpose(1, 0, 2)[None], (8, 8, 32, LENGTH))
    logs = lax.all_to_all(logs, ("upper", "column"), 0, 0, tiled=True)

    return pl.pallas_call(
        final_kernel,
        grid=(4,),
        out_shape=jax.ShapeDtypeStruct((32, 64, LENGTH), jnp.float32),
        in_specs=[
            pl.BlockSpec((8, 64, LENGTH), lambda g: (g, 0, 0)),
            pl.BlockSpec((2, 1, 8, 32, LENGTH), lambda g: (0, g, 0, 0, 0)),
        ],
        out_specs=pl.BlockSpec((8, 64, LENGTH), lambda g: (g, 0, 0)),
        compiler_params=pltpu.CompilerParams(vmem_limit_bytes=16 << 20),
        name="final_kernel",
    )(estimate, logs.reshape(2, 4, 8, 32, LENGTH))


def solution(mesh):
    fine = Mesh(mesh.devices.reshape(2, 4, 32), ("upper", "column", "tile"))
    view = ("upper", "column")
    placed = (P("tile"), P(view, "tile"), P(view), P(view), P(view))
    return jax.shard_map(update, mesh=fine, in_specs=placed, out_specs=P("tile"), check_vma=False)
```

```python
import jax
import jax.numpy as jnp
from jax import lax
from jax.experimental import pallas as pl
from jax.experimental.pallas import tpu as pltpu
from jax.sharding import Mesh, PartitionSpec as P

PROFILE_SIGMA = 48.0
PAIR_SCALE = 32700.0 / 2.8
TOTAL_SCALE = PAIR_SCALE / 4.0
SLABS, ROWS, LENGTH = 32, 32, 256
TOTAL = SLABS * ROWS
GROUP = 8


def blur_matrix(profile):
    column = lax.broadcasted_iota(jnp.int32, (1, LENGTH), 1)
    distance = jnp.minimum(column, LENGTH - column).astype(jnp.float32)
    weights = profile * jnp.exp(-distance * distance / (2.0 * PROFILE_SIGMA * PROFILE_SIGMA))
    kernel = weights / jnp.sum(weights, axis=1, keepdims=True)
    rows = jnp.broadcast_to(kernel, (LENGTH, LENGTH))
    return pltpu.roll(rows, 0, 1, stride=1, stride_axis=0)


def tile_rows(wide, rest, turn, row):
    tiles = pltpu.roll(wide.reshape(-1, 8, LENGTH), turn, 1)
    count = tiles.shape[0]
    tiles = jnp.where(row < 8 - rest, tiles[: count - 1], tiles[1:])
    return tiles.reshape(8 * count - 8, LENGTH)


def blend_of(column, w):
    a = (w * 4 + column + 1).astype(jnp.float32) / 9.0
    return a, 1.0 - a


def place():
    tile = lax.axis_index("tile")
    return lax.axis_index("upper"), lax.axis_index("column"), tile


def pick_kernel(est_ref, out_ref, lines_ref, sem):
    upper, column, tile = place()
    tile_y, tile_z = lax.div(tile, 16), lax.rem(lax.div(tile, 2), 8)
    z = lax.rem(tile_z + column + 4 * upper, 8)
    copies = []
    for k in range(2):
        for u in range(2):
            line = 32 * u + 16 * lax.rem(tile_y + k, 2) + 8 * lax.div(z, 4)
            for h in range(2):
                copy = pltpu.make_async_copy(
                    est_ref.at[:, pl.ds(pl.multiple_of(line, 8), 8), pl.ds(128 * h, 128)],
                    lines_ref.at[k, u, h],
                    sem.at[k, u, h],
                )
                copy.start()
                copies.append(copy)
    rows_ref = lines_ref.reshape(2, 2, 2, ROWS * 8, 128)
    for k in range(2):
        for u in range(2):
            for h in range(2):
                copies[4 * k + 2 * u + h].wait()
                for c in range(2):
                    rows = rows_ref[k, u, h, pl.ds(2 * lax.rem(z, 4) + c, ROWS, stride=8)]
                    out_ref[c, k, u, :, pl.ds(128 * h, 128)] = rows.astype(jnp.bfloat16)


def forward_kernel(
    shift_ref, offset_ref, other_ref, own_profile_ref, other_profile_ref, est0_ref, est1_ref,
    est2_ref, est3_ref, inverse_ref, e_ref,
):
    est_refs = (est0_ref, est1_ref, est2_ref, est3_ref)
    upper, column, tile = place()
    tile_y, tile_z, core = lax.div(tile, 16), lax.rem(lax.div(tile, 2), 8), lax.rem(tile, 2)

    for r, est_ref in enumerate(est_refs):
        source = lax.rem(column + 4 - r, 4)
        for u in range(2):
            z = lax.rem(tile_z + 16 - source - 4 * lax.rem(upper + u, 2), 8)
            for c in range(2):
                for k in range(2):
                    slab = 16 * lax.rem(tile_y + k, 2) + 2 * z + lax.rem(core + c, 2)
                    base = pl.multiple_of(slab * ROWS + 8, 8)
                    e_ref[pl.ds(base, ROWS)] = est_ref[u, k, c].astype(jnp.float32)
    e_ref[pl.ds(0, 8)] = e_ref[pl.ds(TOTAL, 8)]
    e_ref[pl.ds(TOTAL + 8, 16)] = e_ref[pl.ds(8, 16)]
    row = lax.broadcasted_iota(jnp.int32, (1, 8, LENGTH), 1)

    for w in range(2):
        is_own = upper == w
        shift = jnp.where(is_own, shift_ref[0], other_ref[0, LENGTH].astype(jnp.int32))
        offset = jnp.where(is_own, offset_ref[0], other_ref[0, LENGTH + 1].astype(jnp.int32))
        a, b = blend_of(column, w)
        skip = lax.div(8 + offset, 8)
        rest = 8 + offset - 8 * skip
        turn = lax.rem(8 - rest, 8)
        profile = jnp.where(is_own, own_profile_ref[...], other_profile_ref[:, pl.ds(0, LENGTH)])
        matrix = blur_matrix(profile).astype(jnp.bfloat16)

        def blur(k, c, w=w, a=a, b=b, matrix=matrix, skip=skip, rest=rest, turn=turn, shift=shift):
            base = pl.multiple_of(k * (ROWS * GROUP), ROWS * GROUP)
            parts = []
            for q in range(GROUP):
                s = lax.rem(k * GROUP + q + shift, SLABS)
                start = pl.multiple_of(s * ROWS + 8 * skip, 8)
                wide = tile_rows(e_ref[pl.ds(start, ROWS + 16)], rest, turn, row)
                parts.append(a * wide[:ROWS] + b * wide[1 : ROWS + 1])
            warped = jnp.concatenate(parts, axis=0).astype(jnp.bfloat16)
            forward = jnp.dot(warped, matrix, preferred_element_type=jnp.float32)
            inverse_ref[w, pl.ds(base, ROWS * GROUP)] = 1.0 / forward
            return c

        lax.fori_loop(0, SLABS // GROUP, blur, 0)


def back_kernel(
    shift_ref, offset_ref, other_ref, own_profile_ref, other_profile_ref, image_ref, inverse_ref,
    out_ref, b_ref, matrix_ref,
):
    upper, column, _ = place()
    row = lax.broadcasted_iota(jnp.int32, (1, 8, LENGTH), 1)

    for w in range(2):
        profile = jnp.where(upper == w, own_profile_ref[...], other_profile_ref[:, pl.ds(0, LENGTH)])
        matrix_ref[w] = blur_matrix(profile).astype(jnp.bfloat16)
        a, b = blend_of(column, w)

        def blur(k, c, w=w, a=a, b=b):
            base = pl.multiple_of(k * (ROWS * GROUP), ROWS * GROUP)
            edge = pl.multiple_of(lax.rem(base + TOTAL - 8, TOTAL), 8)
            slab = w * SLABS + lax.rem(k * GROUP + SLABS - 1, SLABS)
            image = image_ref[pl.ds(w * SLABS + k * GROUP, GROUP)].reshape(ROWS * GROUP, LENGTH)
            ratios = image.astype(jnp.float32) * inverse_ref[w, pl.ds(base, ROWS * GROUP)]
            before = image_ref[slab, pl.ds(ROWS - 8, 8)].astype(jnp.float32)
            before = before * inverse_ref[w, pl.ds(edge, 8)]
            wide = jnp.concatenate([before, ratios], axis=0)
            blended = a * ratios + b * wide[7 : ROWS * GROUP + 7]
            b_ref[w, pl.ds(base + 8, ROWS * GROUP)] = lax.dot_general(
                blended.astype(jnp.bfloat16),
                matrix_ref[w],
                (((1,), (1,)), ((), ())),
                preferred_element_type=jnp.float32,
            )
            return c

        lax.fori_loop(0, SLABS // GROUP, blur, 0)
        b_ref[w, pl.ds(0, 8)] = b_ref[w, pl.ds(TOTAL, 8)]
        b_ref[w, pl.ds(TOTAL + 8, 8)] = b_ref[w, pl.ds(8, 8)]

    views = []
    for w in range(2):
        is_own = upper == w
        shift = jnp.where(is_own, shift_ref[0], other_ref[0, LENGTH].astype(jnp.int32))
        offset = jnp.where(is_own, offset_ref[0], other_ref[0, LENGTH + 1].astype(jnp.int32))
        skip = lax.div(8 - offset, 8)
        rest = 8 - offset - 8 * skip
        views.append((shift, skip, rest, lax.rem(8 - rest, 8)))

    def join(k, c):
        for q in range(4):
            join_slab(4 * k + q)
        return c

    def join_slab(s):
        product = None
        for w, (shift, skip, rest, turn) in enumerate(views):
            t = lax.rem(s - shift + SLABS, SLABS)
            start = pl.multiple_of(t * ROWS + 8 * skip, 8)
            correction = tile_rows(b_ref[w, pl.ds(start, ROWS + 8)], rest, turn, row)
            product = correction if product is None else product * correction
        code = jnp.round(jnp.log(product) * PAIR_SCALE).astype(jnp.int32).astype(jnp.int16)
        for g in range(4):
            out_ref[lax.rem(g - column + 4, 4), s] = code[8 * g : 8 * g + 8]

    lax.fori_loop(0, SLABS // 4, join, 0)


def final_kernel(est_ref, code_ref, out_ref):
    for h in range(2):
        lines = pl.ds(32 * h, 32)
        logs = code_ref[h, 0].astype(jnp.int32).astype(jnp.float32) * (1.0 / TOTAL_SCALE)
        out_ref[:, lines] = est_ref[:, lines] * jnp.exp(logs)


def distance_route():
    route = []
    for v in range(8):
        for y in range(2):
            for z in range(8):
                for c in range(2):
                    target = 16 * y + 2 * ((z + v) % 8) + c
                    route.append((32 * v + 16 * y + 2 * z + c, 32 * v + target))
    return route


def swap_halves(block, axis, route, keep):
    mine = lax.dynamic_index_in_dim(block, keep, 0, keepdims=False)
    given = lax.dynamic_index_in_dim(block, 1 - keep, 0, keepdims=False)
    return mine, lax.ppermute(given, axis, route)


VMEM = pl.BlockSpec(memory_space=pltpu.VMEM)
SMEM = pl.BlockSpec(memory_space=pltpu.SMEM)


def update(estimate, measured, blur_profile, view_offset, tile_shift):
    upper = lax.axis_index("upper")
    swap = [(0, 1), (1, 0)]
    moves = jnp.concatenate([tile_shift, view_offset]).astype(jnp.float32)
    info = jnp.concatenate([blur_profile, jnp.pad(moves, (0, 126))[None]], axis=1)
    other = lax.ppermute(info, "upper", swap)

    tile = lax.axis_index("tile")
    chip = pl.pallas_call(
        pick_kernel,
        out_shape=jax.ShapeDtypeStruct((2, 2, 2, ROWS, LENGTH), jnp.bfloat16),
        in_specs=[pl.BlockSpec(memory_space=pl.ANY)],
        out_specs=VMEM,
        scratch_shapes=[
            pltpu.VMEM((2, 2, 2, ROWS, 8, 128), jnp.float32),
            pltpu.SemaphoreType.DMA((2, 2, 2)),
        ],
        cost_estimate=pl.CostEstimate(flops=0, bytes_accessed=2 << 20, transcendentals=0),
        compiler_params=pltpu.CompilerParams(vmem_limit_bytes=125 << 19),
        name="pick_kernel",
    )(estimate)
    block = lax.ppermute(chip, ("upper", "column", "tile"), distance_route())
    image = measured[0].transpose(1, 0, 2)
    image_lines = lax.all_to_all(image, ("upper", "tile"), 0, 0, tiled=True)

    pair = swap_halves(block, "tile", [(i, i ^ 1) for i in range(32)], tile % 2)
    block = jnp.stack(pair, axis=2)
    own_line = lax.dynamic_index_in_dim(block, upper, 1, keepdims=False)
    other_line = lax.dynamic_index_in_dim(block, 1 - upper, 1, keepdims=False)
    far = lax.ppermute(other_line[1], ("upper", "tile"), [(i, i ^ 48) for i in range(64)])
    across = lax.ppermute(own_line[1], "tile", [(i, i ^ 16) for i in range(32)])
    beside = lax.ppermute(other_line[0], "upper", swap)
    piece = jnp.stack([own_line[0], across, beside, far]).reshape(2, 2, 2, ROWS, LENGTH)
    est_lines = [piece]
    for d in (1, 2, 3):
        route = [(i, (i + d) % 4) for i in range(4)]
        est_lines.append(lax.ppermute(piece, "column", route))

    inverse = pl.pallas_call(
        forward_kernel,
        out_shape=jax.ShapeDtypeStruct((2, TOTAL, LENGTH), jnp.float32),
        in_specs=[SMEM] * 3 + [VMEM] * 6,
        out_specs=VMEM,
        scratch_shapes=[pltpu.VMEM((TOTAL + 24, LENGTH), jnp.float32)],
        cost_estimate=pl.CostEstimate(
            flops=4 * TOTAL * LENGTH * LENGTH, bytes_accessed=8 << 20, transcendentals=0
        ),
        compiler_params=pltpu.CompilerParams(vmem_limit_bytes=16 << 20),
        name="forward_kernel",
    )(tile_shift, view_offset, other, blur_profile, other, *est_lines)
    codes = pl.pallas_call(
        back_kernel,
        out_shape=jax.ShapeDtypeStruct((4, SLABS, 8, LENGTH), jnp.int16),
        in_specs=[SMEM] * 3 + [VMEM] * 4,
        out_specs=VMEM,
        scratch_shapes=[
            pltpu.VMEM((2, TOTAL + 16, LENGTH), jnp.float32),
            pltpu.VMEM((2, LENGTH, LENGTH), jnp.bfloat16),
        ],
        compiler_params=pltpu.CompilerParams(vmem_limit_bytes=16 << 20),
        name="back_kernel",
    )(tile_shift, view_offset, other, blur_profile, other, image_lines, inverse)
    total = codes[0].astype(jnp.int32)
    for d in (2, 1, 3):
        route = [(i, (i + d) % 4) for i in range(4)]
        total += lax.ppermute(codes[d], "column", route).astype(jnp.int32)
    logs = ((total + 2) >> 2).astype(jnp.int16)
    logs = lax.all_to_all(logs, "tile", 0, 0, tiled=True)
    logs = jnp.broadcast_to(logs.transpose(1, 0, 2)[None], (8, 8, 32, LENGTH))
    logs = lax.all_to_all(logs, ("upper", "column"), 0, 0, tiled=True)

    return pl.pallas_call(
        final_kernel,
        grid=(4,),
        out_shape=jax.ShapeDtypeStruct((32, 64, LENGTH), jnp.float32),
        in_specs=[
            pl.BlockSpec((8, 64, LENGTH), lambda g: (g, 0, 0)),
            pl.BlockSpec((2, 1, 8, 32, LENGTH), lambda g: (0, g, 0, 0, 0)),
        ],
        out_specs=pl.BlockSpec((8, 64, LENGTH), lambda g: (g, 0, 0)),
        compiler_params=pltpu.CompilerParams(vmem_limit_bytes=16 << 20),
        name="final_kernel",
    )(estimate, logs.reshape(2, 4, 8, 32, LENGTH))


def solution(mesh):
    fine = Mesh(mesh.devices.reshape(2, 4, 32), ("upper", "column", "tile"))
    view = ("upper", "column")
    placed = (P("tile"), P(view, "tile"), P(view), P(view), P(view))
    return jax.shard_map(update, mesh=fine, in_specs=placed, out_specs=P("tile"), check_vma=False)
```

```python
import functools

import jax
import jax.numpy as jnp
from jax import lax
from jax.experimental import pallas as pl
from jax.experimental.pallas import tpu as pltpu
from jax.sharding import Mesh, PartitionSpec as P

PROFILE_SIGMA = 48.0
PAIR_SCALE = 32700.0 / 2.8
TOTAL_SCALE = PAIR_SCALE / 4.0
SLABS, ROWS, LENGTH = 32, 32, 256
TOTAL = SLABS * ROWS
GROUP = 8


def blur_matrix(profile):
    column = lax.broadcasted_iota(jnp.int32, (1, LENGTH), 1)
    distance = jnp.minimum(column, LENGTH - column).astype(jnp.float32)
    weights = profile * jnp.exp(-distance * distance / (2.0 * PROFILE_SIGMA * PROFILE_SIGMA))
    kernel = weights / jnp.sum(weights, axis=1, keepdims=True)
    rows = jnp.broadcast_to(kernel, (LENGTH, LENGTH))
    return pltpu.roll(rows, 0, 1, stride=1, stride_axis=0)


def tile_rows(wide, rest, turn, row):
    tiles = pltpu.roll(wide.reshape(-1, 8, LENGTH), turn, 1)
    count = tiles.shape[0]
    tiles = jnp.where(row < 8 - rest, tiles[: count - 1], tiles[1:])
    return tiles.reshape(8 * count - 8, LENGTH)


def blend_of(column, w):
    a = (w * 4 + column + 1).astype(jnp.float32) / 9.0
    return a, 1.0 - a


def place():
    tile = lax.axis_index("tile")
    return lax.axis_index("upper"), lax.axis_index("column"), tile


def pick_kernel(est_ref, out_ref, lines_ref, sem):
    upper, column, tile = place()
    tile_y, tile_z = lax.div(tile, 16), lax.rem(lax.div(tile, 2), 8)
    z = lax.rem(tile_z + column + 4 * upper, 8)
    copies = []
    for k in range(2):
        for u in range(2):
            line = 32 * u + 16 * lax.rem(tile_y + k, 2) + 8 * lax.div(z, 4)
            for h in range(2):
                copy = pltpu.make_async_copy(
                    est_ref.at[:, pl.ds(pl.multiple_of(line, 8), 8), pl.ds(128 * h, 128)],
                    lines_ref.at[k, u, h],
                    sem.at[k, u, h],
                )
                copy.start()
                copies.append(copy)
    rows_ref = lines_ref.reshape(2, 2, 2, ROWS * 8, 128)
    for k in range(2):
        for u in range(2):
            for h in range(2):
                copies[4 * k + 2 * u + h].wait()
                for c in range(2):
                    rows = rows_ref[k, u, h, pl.ds(2 * lax.rem(z, 4) + c, ROWS, stride=8)]
                    out_ref[c, k, u, :, pl.ds(128 * h, 128)] = rows.astype(jnp.bfloat16)


def forward_kernel(
    shift_ref, offset_ref, other_ref, own_profile_ref, other_profile_ref, est0_ref, est1_ref,
    est2_ref, est3_ref, inverse_ref, e_ref,
):
    est_refs = (est0_ref, est1_ref, est2_ref, est3_ref)
    upper, column, tile = place()
    tile_y, tile_z, core = lax.div(tile, 16), lax.rem(lax.div(tile, 2), 8), lax.rem(tile, 2)

    for r, est_ref in enumerate(est_refs):
        source = lax.rem(column + 4 - r, 4)
        for u in range(2):
            z = lax.rem(tile_z + 16 - source - 4 * lax.rem(upper + u, 2), 8)
            for c in range(2):
                for k in range(2):
                    slab = 16 * lax.rem(tile_y + k, 2) + 2 * z + lax.rem(core + c, 2)
                    base = pl.multiple_of(slab * ROWS + 8, 8)
                    e_ref[pl.ds(base, ROWS)] = est_ref[u, k, c].astype(jnp.float32)
    e_ref[pl.ds(0, 8)] = e_ref[pl.ds(TOTAL, 8)]
    e_ref[pl.ds(TOTAL + 8, 16)] = e_ref[pl.ds(8, 16)]
    row = lax.broadcasted_iota(jnp.int32, (1, 8, LENGTH), 1)

    for w in range(2):
        is_own = upper == w
        shift = jnp.where(is_own, shift_ref[0], other_ref[0, LENGTH].astype(jnp.int32))
        offset = jnp.where(is_own, offset_ref[0], other_ref[0, LENGTH + 1].astype(jnp.int32))
        a, b = blend_of(column, w)
        skip = lax.div(8 + offset, 8)
        rest = 8 + offset - 8 * skip
        turn = lax.rem(8 - rest, 8)
        profile = jnp.where(is_own, own_profile_ref[...], other_profile_ref[:, pl.ds(0, LENGTH)])
        matrix = blur_matrix(profile).astype(jnp.bfloat16)

        def blur(k, c, w=w, a=a, b=b, matrix=matrix, skip=skip, rest=rest, turn=turn, shift=shift):
            base = pl.multiple_of(k * (ROWS * GROUP), ROWS * GROUP)
            parts = []
            for q in range(GROUP):
                s = lax.rem(k * GROUP + q + shift, SLABS)
                start = pl.multiple_of(s * ROWS + 8 * skip, 8)
                wide = tile_rows(e_ref[pl.ds(start, ROWS + 16)], rest, turn, row)
                parts.append(a * wide[:ROWS] + b * wide[1 : ROWS + 1])
            warped = jnp.concatenate(parts, axis=0)
            high = warped.astype(jnp.bfloat16)
            low = (warped - high.astype(jnp.float32)).astype(jnp.bfloat16)
            forward = jnp.dot(high, matrix, preferred_element_type=jnp.float32)
            forward += jnp.dot(low, matrix, preferred_element_type=jnp.float32)
            inverse_ref[w, pl.ds(base, ROWS * GROUP)] = 1.0 / forward
            return c

        lax.fori_loop(0, SLABS // GROUP, blur, 0)


def back_kernel(
    shift_ref, offset_ref, other_ref, own_profile_ref, other_profile_ref, image_ref, inverse_ref,
    out_ref, b_ref, matrix_ref,
):
    upper, column, _ = place()
    row = lax.broadcasted_iota(jnp.int32, (1, 8, LENGTH), 1)

    for w in range(2):
        profile = jnp.where(upper == w, own_profile_ref[...], other_profile_ref[:, pl.ds(0, LENGTH)])
        matrix_ref[w] = blur_matrix(profile).astype(jnp.bfloat16)
        a, b = blend_of(column, w)

        def blur(k, c, w=w, a=a, b=b):
            base = pl.multiple_of(k * (ROWS * GROUP), ROWS * GROUP)
            edge = pl.multiple_of(lax.rem(base + TOTAL - 8, TOTAL), 8)
            slab = w * SLABS + lax.rem(k * GROUP + SLABS - 1, SLABS)
            image = image_ref[pl.ds(w * SLABS + k * GROUP, GROUP)].reshape(ROWS * GROUP, LENGTH)
            ratios = image.astype(jnp.float32) * inverse_ref[w, pl.ds(base, ROWS * GROUP)]
            before = image_ref[slab, pl.ds(ROWS - 8, 8)].astype(jnp.float32)
            before = before * inverse_ref[w, pl.ds(edge, 8)]
            wide = jnp.concatenate([before, ratios], axis=0)
            blended = a * ratios + b * wide[7 : ROWS * GROUP + 7]
            b_ref[w, pl.ds(base + 8, ROWS * GROUP)] = lax.dot_general(
                blended.astype(jnp.bfloat16),
                matrix_ref[w],
                (((1,), (1,)), ((), ())),
                preferred_element_type=jnp.float32,
            )
            return c

        lax.fori_loop(0, SLABS // GROUP, blur, 0)
        b_ref[w, pl.ds(0, 8)] = b_ref[w, pl.ds(TOTAL, 8)]
        b_ref[w, pl.ds(TOTAL + 8, 8)] = b_ref[w, pl.ds(8, 8)]

    views = []
    for w in range(2):
        is_own = upper == w
        shift = jnp.where(is_own, shift_ref[0], other_ref[0, LENGTH].astype(jnp.int32))
        offset = jnp.where(is_own, offset_ref[0], other_ref[0, LENGTH + 1].astype(jnp.int32))
        skip = lax.div(8 - offset, 8)
        rest = 8 - offset - 8 * skip
        views.append((shift, skip, rest, lax.rem(8 - rest, 8)))

    def join(k, c):
        for q in range(4):
            join_slab(4 * k + q)
        return c

    def join_slab(s):
        product = None
        for w, (shift, skip, rest, turn) in enumerate(views):
            t = lax.rem(s - shift + SLABS, SLABS)
            start = pl.multiple_of(t * ROWS + 8 * skip, 8)
            correction = tile_rows(b_ref[w, pl.ds(start, ROWS + 8)], rest, turn, row)
            product = correction if product is None else product * correction
        code = jnp.round(jnp.log(product) * PAIR_SCALE).astype(jnp.int32).astype(jnp.int16)
        for g in range(4):
            out_ref[lax.rem(g - column + 4, 4), s] = code[8 * g : 8 * g + 8]

    lax.fori_loop(0, SLABS // 4, join, 0)


def part_of(u, d):
    upper, column, _ = place()
    rows = pl.ds(pl.multiple_of(8 * lax.rem(column - d + 4, 4), 8), 8)
    lines = pl.ds(pl.multiple_of(32 * lax.rem(upper + u, 2), 32), 32)
    return rows, lines


def apply_codes(code_ref, est_ref, part_ref):
    logs = code_ref[...].astype(jnp.int32).astype(jnp.float32) * (1.0 / TOTAL_SCALE)
    part_ref[...] = est_ref[...] * jnp.exp(logs)


def first_kernel(places, later, est_ref, *refs):
    count = len(places)
    codes, (out_ref, rest_ref, parts_ref, in_sem, out_sem) = refs[:count], refs[count:]
    loads, stores = [], []
    for p, (u, d) in enumerate(places + later):
        rows, lines = part_of(u, d)
        target = parts_ref.at[p] if p < count else rest_ref.at[p - count]
        load = pltpu.make_async_copy(est_ref.at[rows, lines], target, in_sem.at[p])
        load.start()
        loads.append(load)
    for p, (u, d) in enumerate(places):
        rows, lines = part_of(u, d)
        loads[p].wait()
        apply_codes(codes[p], parts_ref.at[p], parts_ref.at[count + p])
        store = pltpu.make_async_copy(
            parts_ref.at[count + p], out_ref.at[rows, lines], out_sem.at[p]
        )
        store.start()
        stores.append(store)
    for copy in loads[count:] + stores:
        copy.wait()


def last_kernel(places, est_ref, *refs):
    count = len(places)
    codes, (out_ref, parts_ref, sem) = refs[:count], refs[count + 1 :]
    stores = []
    for p, (u, d) in enumerate(places):
        rows, lines = part_of(u, d)
        apply_codes(codes[p], est_ref.at[p], parts_ref.at[p])
        store = pltpu.make_async_copy(parts_ref.at[p], out_ref.at[rows, lines], sem.at[p])
        store.start()
        stores.append(store)
    for store in stores:
        store.wait()


def finish(places, estimate, pieces, early):
    whole = jax.ShapeDtypeStruct((32, 64, LENGTH), jnp.float32)
    part = (8, 32, LENGTH)
    late = len(places) - early
    first, rest = pl.pallas_call(
        functools.partial(first_kernel, places[:early], places[early:]),
        out_shape=(whole, jax.ShapeDtypeStruct((late, *part), jnp.float32)),
        in_specs=[ANY] + [VMEM] * early,
        out_specs=(ANY, VMEM),
        scratch_shapes=[
            pltpu.VMEM((2 * early, *part), jnp.float32),
            pltpu.SemaphoreType.DMA((early + late,)),
            pltpu.SemaphoreType.DMA((early,)),
        ],
        cost_estimate=pl.CostEstimate(
            flops=early << 17, bytes_accessed=early << 19, transcendentals=early << 16
        ),
        compiler_params=pltpu.CompilerParams(vmem_limit_bytes=32 << 19),
        name="first_kernel",
    )(estimate, *pieces[:early])
    return pl.pallas_call(
        functools.partial(last_kernel, places[early:]),
        out_shape=whole,
        in_specs=[VMEM] * (1 + late) + [ANY],
        out_specs=ANY,
        scratch_shapes=[
            pltpu.VMEM((late, *part), jnp.float32),
            pltpu.SemaphoreType.DMA((late,)),
        ],
        input_output_aliases={1 + late: 0},
        compiler_params=pltpu.CompilerParams(vmem_limit_bytes=16 << 20),
        name="last_kernel",
    )(rest, *pieces[early:], first)


def distance_route():
    route = []
    for v in range(8):
        for y in range(2):
            for z in range(8):
                for c in range(2):
                    target = 16 * y + 2 * ((z + v) % 8) + c
                    route.append((32 * v + 16 * y + 2 * z + c, 32 * v + target))
    return route


def swap_halves(block, axis, route, keep):
    mine = lax.dynamic_index_in_dim(block, keep, 0, keepdims=False)
    given = lax.dynamic_index_in_dim(block, 1 - keep, 0, keepdims=False)
    return mine, lax.ppermute(given, axis, route)


VMEM = pl.BlockSpec(memory_space=pltpu.VMEM)
SMEM = pl.BlockSpec(memory_space=pltpu.SMEM)
ANY = pl.BlockSpec(memory_space=pl.ANY)


def update(estimate, measured, blur_profile, view_offset, tile_shift):
    upper = lax.axis_index("upper")
    swap = [(0, 1), (1, 0)]
    moves = jnp.concatenate([tile_shift, view_offset]).astype(jnp.float32)
    info = jnp.concatenate([blur_profile, jnp.pad(moves, (0, 126))[None]], axis=1)
    other = lax.ppermute(info, "upper", swap)

    tile = lax.axis_index("tile")
    chip = pl.pallas_call(
        pick_kernel,
        out_shape=jax.ShapeDtypeStruct((2, 2, 2, ROWS, LENGTH), jnp.bfloat16),
        in_specs=[pl.BlockSpec(memory_space=pl.ANY)],
        out_specs=VMEM,
        scratch_shapes=[
            pltpu.VMEM((2, 2, 2, ROWS, 8, 128), jnp.float32),
            pltpu.SemaphoreType.DMA((2, 2, 2)),
        ],
        cost_estimate=pl.CostEstimate(flops=0, bytes_accessed=2 << 20, transcendentals=0),
        compiler_params=pltpu.CompilerParams(vmem_limit_bytes=125 << 19),
        name="pick_kernel",
    )(estimate)
    block = lax.ppermute(chip, ("upper", "column", "tile"), distance_route())
    image = measured[0].transpose(1, 0, 2)
    image_lines = lax.all_to_all(image, ("upper", "tile"), 0, 0, tiled=True)

    pair = swap_halves(block, "tile", [(i, i ^ 1) for i in range(32)], tile % 2)
    block = jnp.stack(pair, axis=2)
    own_line = lax.dynamic_index_in_dim(block, upper, 1, keepdims=False)
    other_line = lax.dynamic_index_in_dim(block, 1 - upper, 1, keepdims=False)
    far = lax.ppermute(other_line[1], ("upper", "tile"), [(i, i ^ 48) for i in range(64)])
    across = lax.ppermute(own_line[1], "tile", [(i, i ^ 16) for i in range(32)])
    beside = lax.ppermute(other_line[0], "upper", swap)
    piece = jnp.stack([own_line[0], across, beside, far]).reshape(2, 2, 2, ROWS, LENGTH)
    est_lines = [piece]
    for d in (1, 2, 3):
        route = [(i, (i + d) % 4) for i in range(4)]
        est_lines.append(lax.ppermute(piece, "column", route))

    inverse = pl.pallas_call(
        forward_kernel,
        out_shape=jax.ShapeDtypeStruct((2, TOTAL, LENGTH), jnp.float32),
        in_specs=[SMEM] * 3 + [VMEM] * 6,
        out_specs=VMEM,
        scratch_shapes=[pltpu.VMEM((TOTAL + 24, LENGTH), jnp.float32)],
        cost_estimate=pl.CostEstimate(
            flops=4 * TOTAL * LENGTH * LENGTH, bytes_accessed=8 << 20, transcendentals=0
        ),
        compiler_params=pltpu.CompilerParams(vmem_limit_bytes=16 << 20),
        name="forward_kernel",
    )(tile_shift, view_offset, other, blur_profile, other, *est_lines)
    codes = pl.pallas_call(
        back_kernel,
        out_shape=jax.ShapeDtypeStruct((4, SLABS, 8, LENGTH), jnp.int16),
        in_specs=[SMEM] * 3 + [VMEM] * 4,
        out_specs=VMEM,
        scratch_shapes=[
            pltpu.VMEM((2, TOTAL + 16, LENGTH), jnp.float32),
            pltpu.VMEM((2, LENGTH, LENGTH), jnp.bfloat16),
        ],
        compiler_params=pltpu.CompilerParams(vmem_limit_bytes=16 << 20),
        name="back_kernel",
    )(tile_shift, view_offset, other, blur_profile, other, image_lines, inverse)
    total = codes[0].astype(jnp.int32)
    for d in (2, 1, 3):
        route = [(i, (i + d) % 4) for i in range(4)]
        total += lax.ppermute(codes[d], "column", route).astype(jnp.int32)
    logs = ((total + 2) >> 2).astype(jnp.int16)
    logs = lax.all_to_all(logs, "tile", 0, 0, tiled=True)
    logs = logs.transpose(1, 0, 2)
    places = [(0, 0), (1, 2), (0, 2), (1, 1), (1, 3), (0, 1), (0, 3), (1, 0)]
    pieces = [logs]
    for u, d in places[1:]:
        route = [(i, 4 * ((i // 4 + u) % 2) + (i + d) % 4) for i in range(8)]
        pieces.append(lax.ppermute(logs, ("upper", "column"), route))
    return finish(places, estimate, pieces, 6)


def solution(mesh):
    fine = Mesh(mesh.devices.reshape(2, 4, 32), ("upper", "column", "tile"))
    view = ("upper", "column")
    placed = (P("tile"), P(view, "tile"), P(view), P(view), P(view))
    return jax.shard_map(update, mesh=fine, in_specs=placed, out_specs=P("tile"), check_vma=False)
```

```python
import functools

import jax
import jax.numpy as jnp
from jax import lax
from jax.experimental import pallas as pl
from jax.experimental.pallas import tpu as pltpu
from jax.sharding import Mesh, PartitionSpec as P

PROFILE_SIGMA = 48.0
PAIR_SCALE = 32700.0 / 2.8
TOTAL_SCALE = PAIR_SCALE / 4.0
SLABS, ROWS, LENGTH = 32, 32, 256
TOTAL = SLABS * ROWS
GROUP = 8


def blur_matrix(profile):
    column = lax.broadcasted_iota(jnp.int32, (1, LENGTH), 1)
    distance = jnp.minimum(column, LENGTH - column).astype(jnp.float32)
    weights = profile * jnp.exp(-distance * distance / (2.0 * PROFILE_SIGMA * PROFILE_SIGMA))
    kernel = weights / jnp.sum(weights, axis=1, keepdims=True)
    rows = jnp.broadcast_to(kernel, (LENGTH, LENGTH))
    return pltpu.roll(rows, 0, 1, stride=1, stride_axis=0)


def tile_rows(wide, rest, turn, row):
    tiles = pltpu.roll(wide.reshape(-1, 8, LENGTH), turn, 1)
    count = tiles.shape[0]
    tiles = jnp.where(row < 8 - rest, tiles[: count - 1], tiles[1:])
    return tiles.reshape(8 * count - 8, LENGTH)


def blend_of(column, w):
    a = (w * 4 + column + 1).astype(jnp.float32) / 9.0
    return a, 1.0 - a


def place():
    tile = lax.axis_index("tile")
    return lax.axis_index("upper"), lax.axis_index("column"), tile


def pick_kernel(est_ref, out_ref, lines_ref, sem):
    upper, column, tile = place()
    tile_y, tile_z = lax.div(tile, 16), lax.rem(lax.div(tile, 2), 8)
    z = lax.rem(tile_z + column + 4 * upper, 8)
    copies = []
    for k in range(2):
        for u in range(2):
            line = 32 * u + 16 * lax.rem(tile_y + k, 2) + 8 * lax.div(z, 4)
            for h in range(2):
                copy = pltpu.make_async_copy(
                    est_ref.at[:, pl.ds(pl.multiple_of(line, 8), 8), pl.ds(128 * h, 128)],
                    lines_ref.at[k, u, h],
                    sem.at[k, u, h],
                )
                copy.start()
                copies.append(copy)
    rows_ref = lines_ref.reshape(2, 2, 2, ROWS * 8, 128)
    for k in range(2):
        for u in range(2):
            for h in range(2):
                copies[4 * k + 2 * u + h].wait()
                for c in range(2):
                    rows = rows_ref[k, u, h, pl.ds(2 * lax.rem(z, 4) + c, ROWS, stride=8)]
                    out_ref[c, k, u, :, pl.ds(128 * h, 128)] = rows.astype(jnp.bfloat16)


def forward_kernel(
    shift_ref, offset_ref, other_ref, own_profile_ref, other_profile_ref, est0_ref, est1_ref,
    est2_ref, est3_ref, inverse_ref, e_ref,
):
    est_refs = (est0_ref, est1_ref, est2_ref, est3_ref)
    upper, column, tile = place()
    tile_y, tile_z, core = lax.div(tile, 16), lax.rem(lax.div(tile, 2), 8), lax.rem(tile, 2)

    for r, est_ref in enumerate(est_refs):
        source = lax.rem(column + 4 - r, 4)
        for u in range(2):
            z = lax.rem(tile_z + 16 - source - 4 * lax.rem(upper + u, 2), 8)
            for c in range(2):
                for k in range(2):
                    slab = 16 * lax.rem(tile_y + k, 2) + 2 * z + lax.rem(core + c, 2)
                    base = pl.multiple_of(slab * ROWS + 8, 8)
                    e_ref[pl.ds(base, ROWS)] = est_ref[u, k, c].astype(jnp.float32)
    e_ref[pl.ds(0, 8)] = e_ref[pl.ds(TOTAL, 8)]
    e_ref[pl.ds(TOTAL + 8, 16)] = e_ref[pl.ds(8, 16)]
    row = lax.broadcasted_iota(jnp.int32, (1, 8, LENGTH), 1)

    for w in range(2):
        is_own = upper == w
        shift = jnp.where(is_own, shift_ref[0], other_ref[0, LENGTH].astype(jnp.int32))
        offset = jnp.where(is_own, offset_ref[0], other_ref[0, LENGTH + 1].astype(jnp.int32))
        a, b = blend_of(column, w)
        skip = lax.div(8 + offset, 8)
        rest = 8 + offset - 8 * skip
        turn = lax.rem(8 - rest, 8)
        profile = jnp.where(is_own, own_profile_ref[...], other_profile_ref[:, pl.ds(0, LENGTH)])
        matrix = blur_matrix(profile).astype(jnp.bfloat16)

        def blur(k, c, w=w, a=a, b=b, matrix=matrix, skip=skip, rest=rest, turn=turn, shift=shift):
            base = pl.multiple_of(k * (ROWS * GROUP), ROWS * GROUP)
            parts = []
            for q in range(GROUP):
                s = lax.rem(k * GROUP + q + shift, SLABS)
                start = pl.multiple_of(s * ROWS + 8 * skip, 8)
                wide = tile_rows(e_ref[pl.ds(start, ROWS + 16)], rest, turn, row)
                parts.append(a * wide[:ROWS] + b * wide[1 : ROWS + 1])
            warped = jnp.concatenate(parts, axis=0)
            high = warped.astype(jnp.bfloat16)
            low = (warped - high.astype(jnp.float32)).astype(jnp.bfloat16)
            forward = jnp.dot(high, matrix, preferred_element_type=jnp.float32)
            forward += jnp.dot(low, matrix, preferred_element_type=jnp.float32)
            inverse_ref[w, pl.ds(base, ROWS * GROUP)] = 1.0 / forward
            return c

        lax.fori_loop(0, SLABS // GROUP, blur, 0)


def back_kernel(
    shift_ref, offset_ref, other_ref, own_profile_ref, other_profile_ref, image_ref, inverse_ref,
    out_ref, b_ref, matrix_ref,
):
    upper, column, _ = place()
    row = lax.broadcasted_iota(jnp.int32, (1, 8, LENGTH), 1)

    for w in range(2):
        profile = jnp.where(upper == w, own_profile_ref[...], other_profile_ref[:, pl.ds(0, LENGTH)])
        matrix_ref[w] = blur_matrix(profile).astype(jnp.bfloat16)
        a, b = blend_of(column, w)

        def blur(k, c, w=w, a=a, b=b):
            base = pl.multiple_of(k * (ROWS * GROUP), ROWS * GROUP)
            edge = pl.multiple_of(lax.rem(base + TOTAL - 8, TOTAL), 8)
            slab = w * SLABS + lax.rem(k * GROUP + SLABS - 1, SLABS)
            image = image_ref[pl.ds(w * SLABS + k * GROUP, GROUP)].reshape(ROWS * GROUP, LENGTH)
            ratios = image.astype(jnp.float32) * inverse_ref[w, pl.ds(base, ROWS * GROUP)]
            before = image_ref[slab, pl.ds(ROWS - 8, 8)].astype(jnp.float32)
            before = before * inverse_ref[w, pl.ds(edge, 8)]
            wide = jnp.concatenate([before, ratios], axis=0)
            blended = a * ratios + b * wide[7 : ROWS * GROUP + 7]
            b_ref[w, pl.ds(base + 8, ROWS * GROUP)] = lax.dot_general(
                blended.astype(jnp.bfloat16),
                matrix_ref[w],
                (((1,), (1,)), ((), ())),
                preferred_element_type=jnp.float32,
            )
            return c

        lax.fori_loop(0, SLABS // GROUP, blur, 0)
        b_ref[w, pl.ds(0, 8)] = b_ref[w, pl.ds(TOTAL, 8)]
        b_ref[w, pl.ds(TOTAL + 8, 8)] = b_ref[w, pl.ds(8, 8)]

    views = []
    for w in range(2):
        is_own = upper == w
        shift = jnp.where(is_own, shift_ref[0], other_ref[0, LENGTH].astype(jnp.int32))
        offset = jnp.where(is_own, offset_ref[0], other_ref[0, LENGTH + 1].astype(jnp.int32))
        skip = lax.div(8 - offset, 8)
        rest = 8 - offset - 8 * skip
        views.append((shift, skip, rest, lax.rem(8 - rest, 8)))

    def join(k, c):
        for q in range(4):
            join_slab(4 * k + q)
        return c

    def join_slab(s):
        product = None
        for w, (shift, skip, rest, turn) in enumerate(views):
            t = lax.rem(s - shift + SLABS, SLABS)
            start = pl.multiple_of(t * ROWS + 8 * skip, 8)
            correction = tile_rows(b_ref[w, pl.ds(start, ROWS + 8)], rest, turn, row)
            product = correction if product is None else product * correction
        code = jnp.round(jnp.log(product) * PAIR_SCALE).astype(jnp.int32).astype(jnp.int16)
        for g in range(4):
            out_ref[lax.rem(g - column + 4, 4), s] = code[8 * g : 8 * g + 8]

    lax.fori_loop(0, SLABS // 4, join, 0)


def part_of(u, d):
    upper, column, _ = place()
    rows = pl.ds(pl.multiple_of(8 * lax.rem(column - d + 4, 4), 8), 8)
    lines = pl.ds(pl.multiple_of(32 * lax.rem(upper + u, 2), 32), 32)
    return rows, lines


def apply_codes(code_ref, est_ref, part_ref):
    logs = code_ref[...].astype(jnp.int32).astype(jnp.float32) * (1.0 / TOTAL_SCALE)
    part_ref[...] = est_ref[...] * jnp.exp(logs)


def first_kernel(places, later, est_ref, *refs):
    count = len(places)
    codes, (out_ref, rest_ref, parts_ref, in_sem, out_sem) = refs[:count], refs[count:]
    loads, stores = [], []
    for p, (u, d) in enumerate(places + later):
        rows, lines = part_of(u, d)
        target = parts_ref.at[p] if p < count else rest_ref.at[p - count]
        load = pltpu.make_async_copy(est_ref.at[rows, lines], target, in_sem.at[p])
        load.start()
        loads.append(load)
    for p, (u, d) in enumerate(places):
        rows, lines = part_of(u, d)
        loads[p].wait()
        apply_codes(codes[p], parts_ref.at[p], parts_ref.at[count + p])
        store = pltpu.make_async_copy(
            parts_ref.at[count + p], out_ref.at[rows, lines], out_sem.at[p]
        )
        store.start()
        stores.append(store)
    for copy in loads[count:] + stores:
        copy.wait()


def later_kernel(places, skip, est_ref, *refs):
    count = len(places)
    codes, (out_ref, parts_ref, sem) = refs[:count], refs[count + 1 :]
    stores = []
    for p, (u, d) in enumerate(places):
        rows, lines = part_of(u, d)
        apply_codes(codes[p], est_ref.at[skip + p], parts_ref.at[p])
        store = pltpu.make_async_copy(parts_ref.at[p], out_ref.at[rows, lines], sem.at[p])
        store.start()
        stores.append(store)
    for store in stores:
        store.wait()


def finish(places, estimate, pieces, early, middle):
    whole = jax.ShapeDtypeStruct((32, 64, LENGTH), jnp.float32)
    part = (8, 32, LENGTH)
    late = len(places) - early

    def cost(count):
        return pl.CostEstimate(
            flops=count << 17, bytes_accessed=count << 19, transcendentals=count << 16
        )

    result, rest = pl.pallas_call(
        functools.partial(first_kernel, places[:early], places[early:]),
        out_shape=(whole, jax.ShapeDtypeStruct((late, *part), jnp.float32)),
        in_specs=[ANY] + [VMEM] * early,
        out_specs=(ANY, VMEM),
        scratch_shapes=[
            pltpu.VMEM((2 * early, *part), jnp.float32),
            pltpu.SemaphoreType.DMA((early + late,)),
            pltpu.SemaphoreType.DMA((early,)),
        ],
        cost_estimate=cost(early),
        compiler_params=pltpu.CompilerParams(vmem_limit_bytes=16 << 20),
        name="first_kernel",
    )(estimate, *pieces[:early])
    for start, stop in ((early, early + middle), (early + middle, len(places))):
        count = stop - start
        result = pl.pallas_call(
            functools.partial(later_kernel, places[start:stop], start - early),
            out_shape=whole,
            in_specs=[VMEM] * (1 + count) + [ANY],
            out_specs=ANY,
            scratch_shapes=[
                pltpu.VMEM((count, *part), jnp.float32),
                pltpu.SemaphoreType.DMA((count,)),
            ],
            input_output_aliases={1 + count: 0},
            cost_estimate=cost(count),
            compiler_params=pltpu.CompilerParams(vmem_limit_bytes=16 << 20),
            name="later_kernel",
        )(rest, *pieces[start:stop], result)
    return result


def distance_route():
    route = []
    for v in range(8):
        for y in range(2):
            for z in range(8):
                for c in range(2):
                    target = 16 * y + 2 * ((z + v) % 8) + c
                    route.append((32 * v + 16 * y + 2 * z + c, 32 * v + target))
    return route


def swap_halves(block, axis, route, keep):
    mine = lax.dynamic_index_in_dim(block, keep, 0, keepdims=False)
    given = lax.dynamic_index_in_dim(block, 1 - keep, 0, keepdims=False)
    return mine, lax.ppermute(given, axis, route)


VMEM = pl.BlockSpec(memory_space=pltpu.VMEM)
SMEM = pl.BlockSpec(memory_space=pltpu.SMEM)
ANY = pl.BlockSpec(memory_space=pl.ANY)


def update(estimate, measured, blur_profile, view_offset, tile_shift):
    upper = lax.axis_index("upper")
    swap = [(0, 1), (1, 0)]
    moves = jnp.concatenate([tile_shift, view_offset]).astype(jnp.float32)
    info = jnp.concatenate([blur_profile, jnp.pad(moves, (0, 126))[None]], axis=1)
    other = lax.ppermute(info, "upper", swap)

    tile = lax.axis_index("tile")
    chip = pl.pallas_call(
        pick_kernel,
        out_shape=jax.ShapeDtypeStruct((2, 2, 2, ROWS, LENGTH), jnp.bfloat16),
        in_specs=[pl.BlockSpec(memory_space=pl.ANY)],
        out_specs=VMEM,
        scratch_shapes=[
            pltpu.VMEM((2, 2, 2, ROWS, 8, 128), jnp.float32),
            pltpu.SemaphoreType.DMA((2, 2, 2)),
        ],
        cost_estimate=pl.CostEstimate(flops=0, bytes_accessed=2 << 20, transcendentals=0),
        compiler_params=pltpu.CompilerParams(vmem_limit_bytes=125 << 19),
        name="pick_kernel",
    )(estimate)
    block = lax.ppermute(chip, ("upper", "column", "tile"), distance_route())
    image = measured[0].transpose(1, 0, 2)
    image_lines = lax.all_to_all(image, ("upper", "tile"), 0, 0, tiled=True)

    pair = swap_halves(block, "tile", [(i, i ^ 1) for i in range(32)], tile % 2)
    block = jnp.stack(pair, axis=2)
    own_line = lax.dynamic_index_in_dim(block, upper, 1, keepdims=False)
    other_line = lax.dynamic_index_in_dim(block, 1 - upper, 1, keepdims=False)
    far = lax.ppermute(other_line[1], ("upper", "tile"), [(i, i ^ 48) for i in range(64)])
    across = lax.ppermute(own_line[1], "tile", [(i, i ^ 16) for i in range(32)])
    beside = lax.ppermute(other_line[0], "upper", swap)
    piece = jnp.stack([own_line[0], across, beside, far]).reshape(2, 2, 2, ROWS, LENGTH)
    est_lines = [piece]
    for d in (1, 2, 3):
        route = [(i, (i + d) % 4) for i in range(4)]
        est_lines.append(lax.ppermute(piece, "column", route))

    inverse = pl.pallas_call(
        forward_kernel,
        out_shape=jax.ShapeDtypeStruct((2, TOTAL, LENGTH), jnp.float32),
        in_specs=[SMEM] * 3 + [VMEM] * 6,
        out_specs=VMEM,
        scratch_shapes=[pltpu.VMEM((TOTAL + 24, LENGTH), jnp.float32)],
        cost_estimate=pl.CostEstimate(
            flops=4 * TOTAL * LENGTH * LENGTH, bytes_accessed=8 << 20, transcendentals=0
        ),
        compiler_params=pltpu.CompilerParams(vmem_limit_bytes=16 << 20),
        name="forward_kernel",
    )(tile_shift, view_offset, other, blur_profile, other, *est_lines)
    codes = pl.pallas_call(
        back_kernel,
        out_shape=jax.ShapeDtypeStruct((4, SLABS, 8, LENGTH), jnp.int16),
        in_specs=[SMEM] * 3 + [VMEM] * 4,
        out_specs=VMEM,
        scratch_shapes=[
            pltpu.VMEM((2, TOTAL + 16, LENGTH), jnp.float32),
            pltpu.VMEM((2, LENGTH, LENGTH), jnp.bfloat16),
        ],
        compiler_params=pltpu.CompilerParams(vmem_limit_bytes=16 << 20),
        name="back_kernel",
    )(tile_shift, view_offset, other, blur_profile, other, image_lines, inverse)
    total = codes[0].astype(jnp.int32)
    for d in (2, 1, 3):
        route = [(i, (i + d) % 4) for i in range(4)]
        arrived = lax.ppermute(codes[d], "column", route)
        total += arrived.astype(jnp.int32)
    logs = ((total + 2) >> 2).astype(jnp.int16)
    logs = lax.all_to_all(logs, "tile", 0, 0, tiled=True)
    logs = logs.transpose(1, 0, 2)
    places = [(0, 0), (1, 2), (0, 2), (1, 1), (1, 3), (0, 1), (0, 3), (1, 0)]
    pieces = [logs]
    for u, d in places[1:]:
        route = [(i, 4 * ((i // 4 + u) % 2) + (i + d) % 4) for i in range(8)]
        pieces.append(lax.ppermute(logs, ("upper", "column"), route))
    return finish(places, estimate, pieces, 4, 2)


def solution(mesh):
    fine = Mesh(mesh.devices.reshape(2, 4, 32), ("upper", "column", "tile"))
    view = ("upper", "column")
    placed = (P("tile"), P(view, "tile"), P(view), P(view), P(view))
    return jax.shard_map(update, mesh=fine, in_specs=placed, out_specs=P("tile"), check_vma=False)
```

```python
import functools

import jax
import jax.numpy as jnp
from jax import lax
from jax.experimental import pallas as pl
from jax.experimental.pallas import tpu as pltpu
from jax.sharding import Mesh, PartitionSpec as P

PROFILE_SIGMA = 48.0
PAIR_SCALE = 32700.0 / 2.8
TOTAL_SCALE = PAIR_SCALE / 4.0
SLABS, ROWS, LENGTH = 32, 32, 256
TOTAL = SLABS * ROWS
GROUP = 8


def blur_matrix(profile):
    column = lax.broadcasted_iota(jnp.int32, (1, LENGTH), 1)
    distance = jnp.minimum(column, LENGTH - column).astype(jnp.float32)
    weights = profile * jnp.exp(-distance * distance / (2.0 * PROFILE_SIGMA * PROFILE_SIGMA))
    kernel = weights / jnp.sum(weights, axis=1, keepdims=True)
    rows = jnp.broadcast_to(kernel, (LENGTH, LENGTH))
    return pltpu.roll(rows, 0, 1, stride=1, stride_axis=0)


def tile_rows(wide, rest, turn, row):
    tiles = pltpu.roll(wide.reshape(-1, 8, LENGTH), turn, 1)
    count = tiles.shape[0]
    tiles = jnp.where(row < 8 - rest, tiles[: count - 1], tiles[1:])
    return tiles.reshape(8 * count - 8, LENGTH)


def blend_of(column, w):
    a = (w * 4 + column + 1).astype(jnp.float32) / 9.0
    return a, 1.0 - a


def place():
    tile = lax.axis_index("tile")
    return lax.axis_index("upper"), lax.axis_index("column"), tile


def pick_kernel(
    est_ref, image_ref, out_ref, turned_ref,
    lines_ref, block_ref, wide_ref, part_ref, sem, in_sem, out_sem,
):
    upper, column, tile = place()
    tile_y, tile_z = lax.div(tile, 16), lax.rem(lax.div(tile, 2), 8)
    z = lax.rem(tile_z + column + 4 * upper, 8)
    copies = []
    for k in range(2):
        for u in range(2):
            line = 32 * u + 16 * lax.rem(tile_y + k, 2) + 8 * lax.div(z, 4)
            for h in range(2):
                copy = pltpu.make_async_copy(
                    est_ref.at[:, pl.ds(pl.multiple_of(line, 8), 8), pl.ds(128 * h, 128)],
                    lines_ref.at[k, u, h],
                    sem.at[k, u, h],
                )
                copy.start()
                copies.append(copy)
    loads, stores = [], []
    for j in range(8):
        load = pltpu.make_async_copy(
            image_ref.at[:, pl.ds(8 * j, 8)], block_ref.at[j], in_sem.at[j]
        )
        load.start()
        loads.append(load)
    rows_ref = lines_ref.reshape(2, 2, 2, ROWS * 8, 128)
    for k in range(2):
        for u in range(2):
            for h in range(2):
                copies[4 * k + 2 * u + h].wait()
                for c in range(2):
                    rows = rows_ref[k, u, h, pl.ds(2 * lax.rem(z, 4) + c, ROWS, stride=8)]
                    out_ref[c, k, u, :, pl.ds(128 * h, 128)] = rows.astype(jnp.bfloat16)
    flat_ref = wide_ref.reshape(8, 2, ROWS * 8, 128)
    for j in range(8):
        loads[j].wait()
        for h in range(2):
            lanes = pl.ds(128 * h, 128)
            wide_ref[j, h] = block_ref[j, :, :, lanes].astype(jnp.float32)
            for y in range(8):
                rows = flat_ref[j, h, pl.ds(y, ROWS, stride=8)]
                part_ref[j, y, :, lanes] = rows.astype(jnp.bfloat16)
        store = pltpu.make_async_copy(
            part_ref.at[j], turned_ref.at[pl.ds(8 * j, 8)], out_sem.at[j]
        )
        store.start()
        stores.append(store)
    for store in stores:
        store.wait()


def forward_kernel(
    shift_ref, offset_ref, other_ref, own_profile_ref, other_profile_ref, est0_ref, est1_ref,
    est2_ref, est3_ref, inverse_ref, e_ref,
):
    est_refs = (est0_ref, est1_ref, est2_ref, est3_ref)
    upper, column, tile = place()
    tile_y, tile_z, core = lax.div(tile, 16), lax.rem(lax.div(tile, 2), 8), lax.rem(tile, 2)

    for r, est_ref in enumerate(est_refs):
        source = lax.rem(column + 4 - r, 4)
        for u in range(2):
            z = lax.rem(tile_z + 16 - source - 4 * lax.rem(upper + u, 2), 8)
            for c in range(2):
                for k in range(2):
                    slab = 16 * lax.rem(tile_y + k, 2) + 2 * z + lax.rem(core + c, 2)
                    base = pl.multiple_of(slab * ROWS + 8, 8)
                    e_ref[pl.ds(base, ROWS)] = est_ref[u, k, c].astype(jnp.float32)
    e_ref[pl.ds(0, 8)] = e_ref[pl.ds(TOTAL, 8)]
    e_ref[pl.ds(TOTAL + 8, 16)] = e_ref[pl.ds(8, 16)]
    row = lax.broadcasted_iota(jnp.int32, (1, 8, LENGTH), 1)

    for w in range(2):
        is_own = upper == w
        shift = jnp.where(is_own, shift_ref[0], other_ref[0, LENGTH].astype(jnp.int32))
        offset = jnp.where(is_own, offset_ref[0], other_ref[0, LENGTH + 1].astype(jnp.int32))
        a, b = blend_of(column, w)
        skip = lax.div(8 + offset, 8)
        rest = 8 + offset - 8 * skip
        turn = lax.rem(8 - rest, 8)
        profile = jnp.where(is_own, own_profile_ref[...], other_profile_ref[:, pl.ds(0, LENGTH)])
        matrix = blur_matrix(profile).astype(jnp.bfloat16)

        def blur(k, c, w=w, a=a, b=b, matrix=matrix, skip=skip, rest=rest, turn=turn, shift=shift):
            base = pl.multiple_of(k * (ROWS * GROUP), ROWS * GROUP)
            parts = []
            for q in range(GROUP):
                s = lax.rem(k * GROUP + q + shift, SLABS)
                start = pl.multiple_of(s * ROWS + 8 * skip, 8)
                wide = tile_rows(e_ref[pl.ds(start, ROWS + 16)], rest, turn, row)
                parts.append(a * wide[:ROWS] + b * wide[1 : ROWS + 1])
            warped = jnp.concatenate(parts, axis=0)
            high = warped.astype(jnp.bfloat16)
            low = (warped - high.astype(jnp.float32)).astype(jnp.bfloat16)
            forward = jnp.dot(high, matrix, preferred_element_type=jnp.float32)
            forward += jnp.dot(low, matrix, preferred_element_type=jnp.float32)
            inverse_ref[w, pl.ds(base, ROWS * GROUP)] = 1.0 / forward
            return c

        lax.fori_loop(0, SLABS // GROUP, blur, 0)


def back_kernel(
    shift_ref, offset_ref, other_ref, own_profile_ref, other_profile_ref, image_ref, inverse_ref,
    out_ref, b_ref, matrix_ref,
):
    upper, column, _ = place()
    row = lax.broadcasted_iota(jnp.int32, (1, 8, LENGTH), 1)

    for w in range(2):
        profile = jnp.where(upper == w, own_profile_ref[...], other_profile_ref[:, pl.ds(0, LENGTH)])
        matrix_ref[w] = blur_matrix(profile).astype(jnp.bfloat16)
        a, b = blend_of(column, w)

        def blur(k, c, w=w, a=a, b=b):
            base = pl.multiple_of(k * (ROWS * GROUP), ROWS * GROUP)
            edge = pl.multiple_of(lax.rem(base + TOTAL - 8, TOTAL), 8)
            slab = w * SLABS + lax.rem(k * GROUP + SLABS - 1, SLABS)
            image = image_ref[pl.ds(w * SLABS + k * GROUP, GROUP)].reshape(ROWS * GROUP, LENGTH)
            ratios = image.astype(jnp.float32) * inverse_ref[w, pl.ds(base, ROWS * GROUP)]
            before = image_ref[slab, pl.ds(ROWS - 8, 8)].astype(jnp.float32)
            before = before * inverse_ref[w, pl.ds(edge, 8)]
            wide = jnp.concatenate([before, ratios], axis=0)
            blended = a * ratios + b * wide[7 : ROWS * GROUP + 7]
            b_ref[w, pl.ds(base + 8, ROWS * GROUP)] = lax.dot_general(
                blended.astype(jnp.bfloat16),
                matrix_ref[w],
                (((1,), (1,)), ((), ())),
                preferred_element_type=jnp.float32,
            )
            return c

        lax.fori_loop(0, SLABS // GROUP, blur, 0)
        b_ref[w, pl.ds(0, 8)] = b_ref[w, pl.ds(TOTAL, 8)]
        b_ref[w, pl.ds(TOTAL + 8, 8)] = b_ref[w, pl.ds(8, 8)]

    views = []
    for w in range(2):
        is_own = upper == w
        shift = jnp.where(is_own, shift_ref[0], other_ref[0, LENGTH].astype(jnp.int32))
        offset = jnp.where(is_own, offset_ref[0], other_ref[0, LENGTH + 1].astype(jnp.int32))
        skip = lax.div(8 - offset, 8)
        rest = 8 - offset - 8 * skip
        views.append((shift, skip, rest, lax.rem(8 - rest, 8)))

    def join(k, c):
        for q in range(4):
            join_slab(4 * k + q)
        return c

    def join_slab(s):
        product = None
        for w, (shift, skip, rest, turn) in enumerate(views):
            t = lax.rem(s - shift + SLABS, SLABS)
            start = pl.multiple_of(t * ROWS + 8 * skip, 8)
            correction = tile_rows(b_ref[w, pl.ds(start, ROWS + 8)], rest, turn, row)
            product = correction if product is None else product * correction
        code = jnp.round(jnp.log(product) * PAIR_SCALE).astype(jnp.int32).astype(jnp.int16)
        for g in range(4):
            out_ref[lax.rem(g - column + 4, 4), s] = code[8 * g : 8 * g + 8]

    lax.fori_loop(0, SLABS // 4, join, 0)


def part_of(u, d):
    upper, column, _ = place()
    rows = pl.ds(pl.multiple_of(8 * lax.rem(column - d + 4, 4), 8), 8)
    lines = pl.ds(pl.multiple_of(32 * lax.rem(upper + u, 2), 32), 32)
    return rows, lines


def apply_codes(code_ref, est_ref, part_ref):
    logs = code_ref[...].astype(jnp.int32).astype(jnp.float32) * (1.0 / TOTAL_SCALE)
    part_ref[...] = est_ref[...] * jnp.exp(logs)


def first_kernel(places, later, est_ref, *refs):
    count = len(places)
    codes, (out_ref, rest_ref, parts_ref, in_sem, out_sem) = refs[:count], refs[count:]
    loads, stores = [], []
    for p, (u, d) in enumerate(places + later):
        rows, lines = part_of(u, d)
        target = parts_ref.at[p] if p < count else rest_ref.at[p - count]
        load = pltpu.make_async_copy(est_ref.at[rows, lines], target, in_sem.at[p])
        load.start()
        loads.append(load)
    for p, (u, d) in enumerate(places):
        rows, lines = part_of(u, d)
        loads[p].wait()
        apply_codes(codes[p], parts_ref.at[p], parts_ref.at[count + p])
        store = pltpu.make_async_copy(
            parts_ref.at[count + p], out_ref.at[rows, lines], out_sem.at[p]
        )
        store.start()
        stores.append(store)
    for copy in loads[count:] + stores:
        copy.wait()


def later_kernel(places, skip, est_ref, *refs):
    count = len(places)
    codes, (out_ref, parts_ref, sem) = refs[:count], refs[count + 1 :]
    stores = []
    for p, (u, d) in enumerate(places):
        rows, lines = part_of(u, d)
        apply_codes(codes[p], est_ref.at[skip + p], parts_ref.at[p])
        store = pltpu.make_async_copy(parts_ref.at[p], out_ref.at[rows, lines], sem.at[p])
        store.start()
        stores.append(store)
    for store in stores:
        store.wait()


def finish(places, estimate, pieces, early, middle):
    whole = jax.ShapeDtypeStruct((32, 64, LENGTH), jnp.float32)
    part = (8, 32, LENGTH)
    late = len(places) - early

    def cost(count):
        return pl.CostEstimate(
            flops=count << 17, bytes_accessed=count << 19, transcendentals=count << 16
        )

    result, rest = pl.pallas_call(
        functools.partial(first_kernel, places[:early], places[early:]),
        out_shape=(whole, jax.ShapeDtypeStruct((late, *part), jnp.float32)),
        in_specs=[ANY] + [VMEM] * early,
        out_specs=(ANY, VMEM),
        scratch_shapes=[
            pltpu.VMEM((2 * early, *part), jnp.float32),
            pltpu.SemaphoreType.DMA((early + late,)),
            pltpu.SemaphoreType.DMA((early,)),
        ],
        cost_estimate=cost(early),
        compiler_params=pltpu.CompilerParams(vmem_limit_bytes=16 << 20),
        name="first_kernel",
    )(estimate, *pieces[:early])
    for start, stop in ((early, early + middle), (early + middle, len(places))):
        count = stop - start
        result = pl.pallas_call(
            functools.partial(later_kernel, places[start:stop], start - early),
            out_shape=whole,
            in_specs=[VMEM] * (1 + count) + [ANY],
            out_specs=ANY,
            scratch_shapes=[
                pltpu.VMEM((count, *part), jnp.float32),
                pltpu.SemaphoreType.DMA((count,)),
            ],
            input_output_aliases={1 + count: 0},
            cost_estimate=cost(count),
            compiler_params=pltpu.CompilerParams(vmem_limit_bytes=16 << 20),
            name="later_kernel",
        )(rest, *pieces[start:stop], result)
    return result


def distance_route():
    route = []
    for v in range(8):
        for y in range(2):
            for z in range(8):
                for c in range(2):
                    target = 16 * y + 2 * ((z + v) % 8) + c
                    route.append((32 * v + 16 * y + 2 * z + c, 32 * v + target))
    return route


def swap_halves(block, axis, route, keep):
    mine = lax.dynamic_index_in_dim(block, keep, 0, keepdims=False)
    given = lax.dynamic_index_in_dim(block, 1 - keep, 0, keepdims=False)
    return mine, lax.ppermute(given, axis, route)


VMEM = pl.BlockSpec(memory_space=pltpu.VMEM)
SMEM = pl.BlockSpec(memory_space=pltpu.SMEM)
ANY = pl.BlockSpec(memory_space=pl.ANY)


def update(estimate, measured, blur_profile, view_offset, tile_shift):
    upper = lax.axis_index("upper")
    swap = [(0, 1), (1, 0)]
    moves = jnp.concatenate([tile_shift, view_offset]).astype(jnp.float32)
    info = jnp.concatenate([blur_profile, jnp.pad(moves, (0, 126))[None]], axis=1)
    other = lax.ppermute(info, "upper", swap)

    tile = lax.axis_index("tile")
    chip, image = pl.pallas_call(
        pick_kernel,
        out_shape=(
            jax.ShapeDtypeStruct((2, 2, 2, ROWS, LENGTH), jnp.bfloat16),
            jax.ShapeDtypeStruct((64, ROWS, LENGTH), jnp.bfloat16),
        ),
        in_specs=[ANY, ANY],
        out_specs=(VMEM, ANY),
        scratch_shapes=[
            pltpu.VMEM((2, 2, 2, ROWS, 8, 128), jnp.float32),
            pltpu.VMEM((8, ROWS, 8, LENGTH), jnp.bfloat16),
            pltpu.VMEM((8, 2, ROWS, 8, 128), jnp.float32),
            pltpu.VMEM((8, 8, ROWS, LENGTH), jnp.bfloat16),
            pltpu.SemaphoreType.DMA((2, 2, 2)),
            pltpu.SemaphoreType.DMA((8,)),
            pltpu.SemaphoreType.DMA((8,)),
        ],
        cost_estimate=pl.CostEstimate(flops=0, bytes_accessed=4 << 20, transcendentals=0),
        compiler_params=pltpu.CompilerParams(vmem_limit_bytes=125 << 19),
        name="pick_kernel",
    )(estimate, measured[0])
    block = lax.ppermute(chip, ("upper", "column", "tile"), distance_route())
    image_lines = lax.all_to_all(image, ("upper", "tile"), 0, 0, tiled=True)

    pair = swap_halves(block, "tile", [(i, i ^ 1) for i in range(32)], tile % 2)
    block = jnp.stack(pair, axis=2)
    own_line = lax.dynamic_index_in_dim(block, upper, 1, keepdims=False)
    other_line = lax.dynamic_index_in_dim(block, 1 - upper, 1, keepdims=False)
    far = lax.ppermute(other_line[1], ("upper", "tile"), [(i, i ^ 48) for i in range(64)])
    across = lax.ppermute(own_line[1], "tile", [(i, i ^ 16) for i in range(32)])
    beside = lax.ppermute(other_line[0], "upper", swap)
    piece = jnp.stack([own_line[0], across, beside, far]).reshape(2, 2, 2, ROWS, LENGTH)
    est_lines = [piece]
    for d in (1, 2, 3):
        route = [(i, (i + d) % 4) for i in range(4)]
        est_lines.append(lax.ppermute(piece, "column", route))

    inverse = pl.pallas_call(
        forward_kernel,
        out_shape=jax.ShapeDtypeStruct((2, TOTAL, LENGTH), jnp.float32),
        in_specs=[SMEM] * 3 + [VMEM] * 6,
        out_specs=VMEM,
        scratch_shapes=[pltpu.VMEM((TOTAL + 24, LENGTH), jnp.float32)],
        cost_estimate=pl.CostEstimate(
            flops=4 * TOTAL * LENGTH * LENGTH, bytes_accessed=8 << 20, transcendentals=0
        ),
        compiler_params=pltpu.CompilerParams(vmem_limit_bytes=16 << 20),
        name="forward_kernel",
    )(tile_shift, view_offset, other, blur_profile, other, *est_lines)
    codes = pl.pallas_call(
        back_kernel,
        out_shape=jax.ShapeDtypeStruct((4, SLABS, 8, LENGTH), jnp.int16),
        in_specs=[SMEM] * 3 + [VMEM] * 4,
        out_specs=VMEM,
        scratch_shapes=[
            pltpu.VMEM((2, TOTAL + 16, LENGTH), jnp.float32),
            pltpu.VMEM((2, LENGTH, LENGTH), jnp.bfloat16),
        ],
        compiler_params=pltpu.CompilerParams(vmem_limit_bytes=16 << 20),
        name="back_kernel",
    )(tile_shift, view_offset, other, blur_profile, other, image_lines, inverse)
    total = codes[0].astype(jnp.int32)
    for d in (2, 1, 3):
        route = [(i, (i + d) % 4) for i in range(4)]
        arrived = lax.ppermute(codes[d], "column", route)
        total += arrived.astype(jnp.int32)
    logs = ((total + 2) >> 2).astype(jnp.int16)
    logs = lax.all_to_all(logs, "tile", 0, 0, tiled=True)
    logs = logs.transpose(1, 0, 2)
    partner = lax.ppermute(logs, "upper", swap)
    places, pieces = [(0, 0), (1, 0)], [logs, partner]
    for u, d in [(0, 2), (0, 1), (0, 3), (1, 2), (1, 1), (1, 3)]:
        route = [(i, (i + d) % 4) for i in range(4)]
        places.append((u, d))
        pieces.append(lax.ppermute(pieces[u], "column", route))
    return finish(places, estimate, pieces, 4, 2)


def solution(mesh):
    fine = Mesh(mesh.devices.reshape(2, 4, 32), ("upper", "column", "tile"))
    view = ("upper", "column")
    placed = (P("tile"), P(view, "tile"), P(view), P(view), P(view))
    return jax.shard_map(update, mesh=fine, in_specs=placed, out_specs=P("tile"), check_vma=False)
```

```python
import functools

import jax
import jax.numpy as jnp
from jax import lax
from jax.experimental import pallas as pl
from jax.experimental.pallas import tpu as pltpu
from jax.sharding import Mesh, PartitionSpec as P

PROFILE_SIGMA = 48.0
PAIR_SCALE = 32700.0 / 2.8
TOTAL_SCALE = PAIR_SCALE / 4.0
SLABS, ROWS, LENGTH = 32, 32, 256
TOTAL = SLABS * ROWS
GROUP = 8


def blur_matrix(profile):
    column = lax.broadcasted_iota(jnp.int32, (1, LENGTH), 1)
    distance = jnp.minimum(column, LENGTH - column).astype(jnp.float32)
    weights = profile * jnp.exp(-distance * distance / (2.0 * PROFILE_SIGMA * PROFILE_SIGMA))
    kernel = weights / jnp.sum(weights, axis=1, keepdims=True)
    rows = jnp.broadcast_to(kernel, (LENGTH, LENGTH))
    return pltpu.roll(rows, 0, 1, stride=1, stride_axis=0)


def tile_rows(wide, rest, turn, row):
    tiles = pltpu.roll(wide.reshape(-1, 8, LENGTH), turn, 1)
    count = tiles.shape[0]
    tiles = jnp.where(row < 8 - rest, tiles[: count - 1], tiles[1:])
    return tiles.reshape(8 * count - 8, LENGTH)


def blend_of(column, w):
    a = (w * 4 + column + 1).astype(jnp.float32) / 9.0
    return a, 1.0 - a


def place():
    tile = lax.axis_index("tile")
    return lax.axis_index("upper"), lax.axis_index("column"), tile


def pick_kernel(est_ref, out_ref, lines_ref, sem):
    upper, column, tile = place()
    tile_y, tile_z = lax.div(tile, 16), lax.rem(lax.div(tile, 2), 8)
    z = lax.rem(tile_z + column + 4 * upper, 8)
    copies = []
    for k in range(2):
        for u in range(2):
            line = 32 * u + 16 * lax.rem(tile_y + k, 2) + 8 * lax.div(z, 4)
            for h in range(2):
                copy = pltpu.make_async_copy(
                    est_ref.at[:, pl.ds(pl.multiple_of(line, 8), 8), pl.ds(128 * h, 128)],
                    lines_ref.at[k, u, h],
                    sem.at[k, u, h],
                )
                copy.start()
                copies.append(copy)
    rows_ref = lines_ref.reshape(2, 2, 2, ROWS * 8, 128)
    for k in range(2):
        for u in range(2):
            for h in range(2):
                copies[4 * k + 2 * u + h].wait()
                for c in range(2):
                    rows = rows_ref[k, u, h, pl.ds(2 * lax.rem(z, 4) + c, ROWS, stride=8)]
                    out_ref[c, k, u, :, pl.ds(128 * h, 128)] = rows.astype(jnp.bfloat16)


def forward_kernel(
    shift_ref, offset_ref, other_ref, own_profile_ref, other_profile_ref, est0_ref, est1_ref,
    est2_ref, est3_ref, inverse_ref, e_ref,
):
    est_refs = (est0_ref, est1_ref, est2_ref, est3_ref)
    upper, column, tile = place()
    tile_y, tile_z, core = lax.div(tile, 16), lax.rem(lax.div(tile, 2), 8), lax.rem(tile, 2)

    for r, est_ref in enumerate(est_refs):
        source = lax.rem(column + 4 - r, 4)
        for u in range(2):
            z = lax.rem(tile_z + 16 - source - 4 * lax.rem(upper + u, 2), 8)
            for c in range(2):
                for k in range(2):
                    slab = 16 * lax.rem(tile_y + k, 2) + 2 * z + lax.rem(core + c, 2)
                    base = pl.multiple_of(slab * ROWS + 8, 8)
                    e_ref[pl.ds(base, ROWS)] = est_ref[u, k, c].astype(jnp.float32)
    e_ref[pl.ds(0, 8)] = e_ref[pl.ds(TOTAL, 8)]
    e_ref[pl.ds(TOTAL + 8, 16)] = e_ref[pl.ds(8, 16)]
    row = lax.broadcasted_iota(jnp.int32, (1, 8, LENGTH), 1)

    for w in range(2):
        is_own = upper == w
        shift = jnp.where(is_own, shift_ref[0], other_ref[0, LENGTH].astype(jnp.int32))
        offset = jnp.where(is_own, offset_ref[0], other_ref[0, LENGTH + 1].astype(jnp.int32))
        a, b = blend_of(column, w)
        skip = lax.div(8 + offset, 8)
        rest = 8 + offset - 8 * skip
        turn = lax.rem(8 - rest, 8)
        profile = jnp.where(is_own, own_profile_ref[...], other_profile_ref[:, pl.ds(0, LENGTH)])
        matrix = blur_matrix(profile).astype(jnp.bfloat16)

        def blur(k, c, w=w, a=a, b=b, matrix=matrix, skip=skip, rest=rest, turn=turn, shift=shift):
            base = pl.multiple_of(k * (ROWS * GROUP), ROWS * GROUP)
            parts = []
            for q in range(GROUP):
                s = lax.rem(k * GROUP + q + shift, SLABS)
                start = pl.multiple_of(s * ROWS + 8 * skip, 8)
                wide = tile_rows(e_ref[pl.ds(start, ROWS + 16)], rest, turn, row)
                parts.append(a * wide[:ROWS] + b * wide[1 : ROWS + 1])
            warped = jnp.concatenate(parts, axis=0)
            high = warped.astype(jnp.bfloat16)
            low = (warped - high.astype(jnp.float32)).astype(jnp.bfloat16)
            forward = jnp.dot(high, matrix, preferred_element_type=jnp.float32)
            forward += jnp.dot(low, matrix, preferred_element_type=jnp.float32)
            inverse_ref[w, pl.ds(base, ROWS * GROUP)] = 1.0 / forward
            return c

        lax.fori_loop(0, SLABS // GROUP, blur, 0)


def back_kernel(
    shift_ref, offset_ref, other_ref, own_profile_ref, other_profile_ref, image_ref, inverse_ref,
    out_ref, b_ref, matrix_ref,
):
    upper, column, _ = place()
    row = lax.broadcasted_iota(jnp.int32, (1, 8, LENGTH), 1)

    for w in range(2):
        profile = jnp.where(upper == w, own_profile_ref[...], other_profile_ref[:, pl.ds(0, LENGTH)])
        matrix_ref[w] = blur_matrix(profile).astype(jnp.bfloat16)
        a, b = blend_of(column, w)

        def blur(k, c, w=w, a=a, b=b):
            base = pl.multiple_of(k * (ROWS * GROUP), ROWS * GROUP)
            edge = pl.multiple_of(lax.rem(base + TOTAL - 8, TOTAL), 8)
            slab = w * SLABS + lax.rem(k * GROUP + SLABS - 1, SLABS)
            image = image_ref[pl.ds(w * SLABS + k * GROUP, GROUP)].reshape(ROWS * GROUP, LENGTH)
            ratios = image.astype(jnp.float32) * inverse_ref[w, pl.ds(base, ROWS * GROUP)]
            before = image_ref[slab, pl.ds(ROWS - 8, 8)].astype(jnp.float32)
            before = before * inverse_ref[w, pl.ds(edge, 8)]
            wide = jnp.concatenate([before, ratios], axis=0)
            blended = a * ratios + b * wide[7 : ROWS * GROUP + 7]
            b_ref[w, pl.ds(base + 8, ROWS * GROUP)] = lax.dot_general(
                blended.astype(jnp.bfloat16),
                matrix_ref[w],
                (((1,), (1,)), ((), ())),
                preferred_element_type=jnp.float32,
            )
            return c

        lax.fori_loop(0, SLABS // GROUP, blur, 0)
        b_ref[w, pl.ds(0, 8)] = b_ref[w, pl.ds(TOTAL, 8)]
        b_ref[w, pl.ds(TOTAL + 8, 8)] = b_ref[w, pl.ds(8, 8)]

    views = []
    for w in range(2):
        is_own = upper == w
        shift = jnp.where(is_own, shift_ref[0], other_ref[0, LENGTH].astype(jnp.int32))
        offset = jnp.where(is_own, offset_ref[0], other_ref[0, LENGTH + 1].astype(jnp.int32))
        skip = lax.div(8 - offset, 8)
        rest = 8 - offset - 8 * skip
        views.append((shift, skip, rest, lax.rem(8 - rest, 8)))

    def join(k, c):
        for q in range(4):
            join_slab(4 * k + q)
        return c

    def join_slab(s):
        product = None
        for w, (shift, skip, rest, turn) in enumerate(views):
            t = lax.rem(s - shift + SLABS, SLABS)
            start = pl.multiple_of(t * ROWS + 8 * skip, 8)
            correction = tile_rows(b_ref[w, pl.ds(start, ROWS + 8)], rest, turn, row)
            product = correction if product is None else product * correction
        code = jnp.round(jnp.log(product) * PAIR_SCALE).astype(jnp.int32).astype(jnp.int16)
        for g in range(4):
            out_ref[lax.rem(g - column + 4, 4), s] = code[8 * g : 8 * g + 8]

    lax.fori_loop(0, SLABS // 4, join, 0)


def part_of(u, d):
    upper, column, _ = place()
    rows = pl.ds(pl.multiple_of(8 * lax.rem(column - d + 4, 4), 8), 8)
    lines = pl.ds(pl.multiple_of(32 * lax.rem(upper + u, 2), 32), 32)
    return rows, lines


def apply_codes(code_ref, est_ref, part_ref):
    logs = code_ref[...].astype(jnp.int32).astype(jnp.float32) * (1.0 / TOTAL_SCALE)
    part_ref[...] = est_ref[...] * jnp.exp(logs)


def first_kernel(places, later, est_ref, *refs):
    count = len(places)
    codes, (out_ref, rest_ref, parts_ref, in_sem, out_sem) = refs[:count], refs[count:]
    loads, stores = [], []
    for p, (u, d) in enumerate(places + later):
        rows, lines = part_of(u, d)
        target = parts_ref.at[p] if p < count else rest_ref.at[p - count]
        load = pltpu.make_async_copy(est_ref.at[rows, lines], target, in_sem.at[p])
        load.start()
        loads.append(load)
    for p, (u, d) in enumerate(places):
        rows, lines = part_of(u, d)
        loads[p].wait()
        apply_codes(codes[p], parts_ref.at[p], parts_ref.at[count + p])
        store = pltpu.make_async_copy(
            parts_ref.at[count + p], out_ref.at[rows, lines], out_sem.at[p]
        )
        store.start()
        stores.append(store)
    for copy in loads[count:] + stores:
        copy.wait()


def later_kernel(places, skip, est_ref, *refs):
    count = len(places)
    codes, (out_ref, parts_ref, sem) = refs[:count], refs[count + 1 :]
    stores = []
    for p, (u, d) in enumerate(places):
        rows, lines = part_of(u, d)
        apply_codes(codes[p], est_ref.at[skip + p], parts_ref.at[p])
        store = pltpu.make_async_copy(parts_ref.at[p], out_ref.at[rows, lines], sem.at[p])
        store.start()
        stores.append(store)
    for store in stores:
        store.wait()


def finish(places, estimate, pieces, early, middle):
    whole = jax.ShapeDtypeStruct((32, 64, LENGTH), jnp.float32)
    part = (8, 32, LENGTH)
    late = len(places) - early

    def cost(count):
        return pl.CostEstimate(
            flops=count << 17, bytes_accessed=count << 19, transcendentals=count << 16
        )

    result, rest = pl.pallas_call(
        functools.partial(first_kernel, places[:early], places[early:]),
        out_shape=(whole, jax.ShapeDtypeStruct((late, *part), jnp.float32)),
        in_specs=[ANY] + [VMEM] * early,
        out_specs=(ANY, VMEM),
        scratch_shapes=[
            pltpu.VMEM((2 * early, *part), jnp.float32),
            pltpu.SemaphoreType.DMA((early + late,)),
            pltpu.SemaphoreType.DMA((early,)),
        ],
        cost_estimate=cost(early),
        compiler_params=pltpu.CompilerParams(vmem_limit_bytes=16 << 20),
        name="first_kernel",
    )(estimate, *pieces[:early])
    for start, stop in ((early, early + middle), (early + middle, len(places))):
        count = stop - start
        result = pl.pallas_call(
            functools.partial(later_kernel, places[start:stop], start - early),
            out_shape=whole,
            in_specs=[VMEM] * (1 + count) + [ANY],
            out_specs=ANY,
            scratch_shapes=[
                pltpu.VMEM((count, *part), jnp.float32),
                pltpu.SemaphoreType.DMA((count,)),
            ],
            input_output_aliases={1 + count: 0},
            cost_estimate=cost(count),
            compiler_params=pltpu.CompilerParams(vmem_limit_bytes=16 << 20),
            name="later_kernel",
        )(rest, *pieces[start:stop], result)
    return result


def distance_route():
    route = []
    for v in range(8):
        for y in range(2):
            for z in range(8):
                for c in range(2):
                    target = 16 * y + 2 * ((z + v) % 8) + c
                    route.append((32 * v + 16 * y + 2 * z + c, 32 * v + target))
    return route


def swap_halves(block, axis, route, keep):
    mine = lax.dynamic_index_in_dim(block, keep, 0, keepdims=False)
    given = lax.dynamic_index_in_dim(block, 1 - keep, 0, keepdims=False)
    return mine, lax.ppermute(given, axis, route)


VMEM = pl.BlockSpec(memory_space=pltpu.VMEM)
SMEM = pl.BlockSpec(memory_space=pltpu.SMEM)
ANY = pl.BlockSpec(memory_space=pl.ANY)


def update(estimate, measured, blur_profile, view_offset, tile_shift):
    upper = lax.axis_index("upper")
    swap = [(0, 1), (1, 0)]
    moves = jnp.concatenate([tile_shift, view_offset]).astype(jnp.float32)
    info = jnp.concatenate([blur_profile, jnp.pad(moves, (0, 126))[None]], axis=1)
    other = lax.ppermute(info, "upper", swap)

    tile = lax.axis_index("tile")
    chip = pl.pallas_call(
        pick_kernel,
        out_shape=jax.ShapeDtypeStruct((2, 2, 2, ROWS, LENGTH), jnp.bfloat16),
        in_specs=[pl.BlockSpec(memory_space=pl.ANY)],
        out_specs=VMEM,
        scratch_shapes=[
            pltpu.VMEM((2, 2, 2, ROWS, 8, 128), jnp.float32),
            pltpu.SemaphoreType.DMA((2, 2, 2)),
        ],
        cost_estimate=pl.CostEstimate(flops=0, bytes_accessed=2 << 20, transcendentals=0),
        compiler_params=pltpu.CompilerParams(vmem_limit_bytes=125 << 19),
        name="pick_kernel",
    )(estimate)
    block = lax.ppermute(chip, ("upper", "column", "tile"), distance_route())
    image = measured[0].transpose(1, 0, 2)
    image_lines = lax.all_to_all(image, ("upper", "tile"), 0, 0, tiled=True)

    pair = swap_halves(block, "tile", [(i, i ^ 1) for i in range(32)], tile % 2)
    block = jnp.stack(pair, axis=2)
    own_line = lax.dynamic_index_in_dim(block, upper, 1, keepdims=False)
    other_line = lax.dynamic_index_in_dim(block, 1 - upper, 1, keepdims=False)
    far = lax.ppermute(other_line[1], ("upper", "tile"), [(i, i ^ 48) for i in range(64)])
    across = lax.ppermute(own_line[1], "tile", [(i, i ^ 16) for i in range(32)])
    beside = lax.ppermute(other_line[0], "upper", swap)
    piece = jnp.stack([own_line[0], across, beside, far]).reshape(2, 2, 2, ROWS, LENGTH)
    est_lines = [piece]
    for d in (1, 2, 3):
        route = [(i, (i + d) % 4) for i in range(4)]
        est_lines.append(lax.ppermute(piece, "column", route))

    inverse = pl.pallas_call(
        forward_kernel,
        out_shape=jax.ShapeDtypeStruct((2, TOTAL, LENGTH), jnp.float32),
        in_specs=[SMEM] * 3 + [VMEM] * 6,
        out_specs=VMEM,
        scratch_shapes=[pltpu.VMEM((TOTAL + 24, LENGTH), jnp.float32)],
        cost_estimate=pl.CostEstimate(
            flops=4 * TOTAL * LENGTH * LENGTH, bytes_accessed=8 << 20, transcendentals=0
        ),
        compiler_params=pltpu.CompilerParams(vmem_limit_bytes=16 << 20),
        name="forward_kernel",
    )(tile_shift, view_offset, other, blur_profile, other, *est_lines)
    codes = pl.pallas_call(
        back_kernel,
        out_shape=jax.ShapeDtypeStruct((4, SLABS, 8, LENGTH), jnp.int16),
        in_specs=[SMEM] * 3 + [VMEM] * 4,
        out_specs=VMEM,
        scratch_shapes=[
            pltpu.VMEM((2, TOTAL + 16, LENGTH), jnp.float32),
            pltpu.VMEM((2, LENGTH, LENGTH), jnp.bfloat16),
        ],
        compiler_params=pltpu.CompilerParams(vmem_limit_bytes=16 << 20),
        name="back_kernel",
    )(tile_shift, view_offset, other, blur_profile, other, image_lines, inverse)
    total = codes[0].astype(jnp.int32)
    for d in (2, 1, 3):
        route = [(i, (i + d) % 4) for i in range(4)]
        arrived = lax.ppermute(codes[d], "column", route)
        total += arrived.astype(jnp.int32)
    logs = ((total + 2) >> 2).astype(jnp.int16)
    logs = lax.all_to_all(logs, "tile", 0, 0, tiled=True)
    logs = logs.transpose(1, 0, 2)
    partner = lax.ppermute(logs, "upper", swap)

    def give(piece, d):
        return lax.ppermute(piece, "column", [(i, (i + d) % 4) for i in range(4)])

    pieces = {(0, 0): logs, (1, 0): partner}
    pieces[0, 1] = give(logs, 1)
    pieces[0, 3] = give(logs, 3)
    both = give(jnp.stack([logs, partner]), 2)
    pieces[1, 1] = give(partner, 1)
    pieces[1, 3] = give(partner, 3)
    pieces[0, 2], pieces[1, 2] = both[0], both[1]
    return finish(list(pieces), estimate, list(pieces.values()), 4, 2)


def solution(mesh):
    fine = Mesh(mesh.devices.reshape(2, 4, 32), ("upper", "column", "tile"))
    view = ("upper", "column")
    placed = (P("tile"), P(view, "tile"), P(view), P(view), P(view))
    return jax.shard_map(update, mesh=fine, in_specs=placed, out_specs=P("tile"), check_vma=False)
```

```python
import functools

import jax
import jax.numpy as jnp
from jax import lax
from jax.experimental import pallas as pl
from jax.experimental.pallas import tpu as pltpu
from jax.sharding import Mesh, PartitionSpec as P

PROFILE_SIGMA = 48.0
PAIR_SCALE = 32700.0 / 2.8
TOTAL_SCALE = PAIR_SCALE / 4.0
SLABS, ROWS, LENGTH = 32, 32, 256
TOTAL = SLABS * ROWS
GROUP = 8


def blur_matrix(profile):
    column = lax.broadcasted_iota(jnp.int32, (1, LENGTH), 1)
    distance = jnp.minimum(column, LENGTH - column).astype(jnp.float32)
    weights = profile * jnp.exp(-distance * distance / (2.0 * PROFILE_SIGMA * PROFILE_SIGMA))
    kernel = weights / jnp.sum(weights, axis=1, keepdims=True)
    rows = jnp.broadcast_to(kernel, (LENGTH, LENGTH))
    return pltpu.roll(rows, 0, 1, stride=1, stride_axis=0)


def tile_rows(wide, rest, turn, row):
    tiles = pltpu.roll(wide.reshape(-1, 8, LENGTH), turn, 1)
    count = tiles.shape[0]
    tiles = jnp.where(row < 8 - rest, tiles[: count - 1], tiles[1:])
    return tiles.reshape(8 * count - 8, LENGTH)


def blend_of(column, w):
    a = (w * 4 + column + 1).astype(jnp.float32) / 9.0
    return a, 1.0 - a


def place():
    tile = lax.axis_index("tile")
    return lax.axis_index("upper"), lax.axis_index("column"), tile


def pick_kernel(est_ref, out_ref, lines_ref, sem):
    upper, column, tile = place()
    tile_y, tile_z = lax.div(tile, 16), lax.rem(lax.div(tile, 2), 8)
    z = lax.rem(tile_z + column + 4 * upper, 8)
    copies = []
    for k in range(2):
        for u in range(2):
            line = 32 * u + 16 * lax.rem(tile_y + k, 2) + 8 * lax.div(z, 4)
            for h in range(2):
                copy = pltpu.make_async_copy(
                    est_ref.at[:, pl.ds(pl.multiple_of(line, 8), 8), pl.ds(128 * h, 128)],
                    lines_ref.at[k, u, h],
                    sem.at[k, u, h],
                )
                copy.start()
                copies.append(copy)
    rows_ref = lines_ref.reshape(2, 2, 2, ROWS * 8, 128)
    for k in range(2):
        for u in range(2):
            for h in range(2):
                copies[4 * k + 2 * u + h].wait()
                for c in range(2):
                    rows = rows_ref[k, u, h, pl.ds(2 * lax.rem(z, 4) + c, ROWS, stride=8)]
                    out_ref[c, k, u, :, pl.ds(128 * h, 128)] = rows.astype(jnp.bfloat16)


def forward_kernel(
    shift_ref, offset_ref, other_ref, own_profile_ref, other_profile_ref, est0_ref, est1_ref,
    est2_ref, est3_ref, inverse_ref, e_ref,
):
    est_refs = (est0_ref, est1_ref, est2_ref, est3_ref)
    upper, column, tile = place()
    tile_y, tile_z, core = lax.div(tile, 16), lax.rem(lax.div(tile, 2), 8), lax.rem(tile, 2)

    for r, est_ref in enumerate(est_refs):
        source = lax.rem(column + 4 - r, 4)
        for u in range(2):
            z = lax.rem(tile_z + 16 - source - 4 * lax.rem(upper + u, 2), 8)
            for c in range(2):
                for k in range(2):
                    slab = 16 * lax.rem(tile_y + k, 2) + 2 * z + lax.rem(core + c, 2)
                    base = pl.multiple_of(slab * ROWS + 8, 8)
                    e_ref[pl.ds(base, ROWS)] = est_ref[u, k, c].astype(jnp.float32)
    e_ref[pl.ds(0, 8)] = e_ref[pl.ds(TOTAL, 8)]
    e_ref[pl.ds(TOTAL + 8, 16)] = e_ref[pl.ds(8, 16)]
    row = lax.broadcasted_iota(jnp.int32, (1, 8, LENGTH), 1)

    for w in range(2):
        is_own = upper == w
        shift = jnp.where(is_own, shift_ref[0], other_ref[0, LENGTH].astype(jnp.int32))
        offset = jnp.where(is_own, offset_ref[0], other_ref[0, LENGTH + 1].astype(jnp.int32))
        a, b = blend_of(column, w)
        skip = lax.div(8 + offset, 8)
        rest = 8 + offset - 8 * skip
        turn = lax.rem(8 - rest, 8)
        profile = jnp.where(is_own, own_profile_ref[...], other_profile_ref[:, pl.ds(0, LENGTH)])
        matrix = blur_matrix(profile).astype(jnp.bfloat16)

        def blur(k, c, w=w, a=a, b=b, matrix=matrix, skip=skip, rest=rest, turn=turn, shift=shift):
            base = pl.multiple_of(k * (ROWS * GROUP), ROWS * GROUP)
            parts = []
            for q in range(GROUP):
                s = lax.rem(k * GROUP + q + shift, SLABS)
                start = pl.multiple_of(s * ROWS + 8 * skip, 8)
                wide = tile_rows(e_ref[pl.ds(start, ROWS + 16)], rest, turn, row)
                parts.append(a * wide[:ROWS] + b * wide[1 : ROWS + 1])
            warped = jnp.concatenate(parts, axis=0)
            high = warped.astype(jnp.bfloat16)
            low = (warped - high.astype(jnp.float32)).astype(jnp.bfloat16)
            forward = jnp.dot(high, matrix, preferred_element_type=jnp.float32)
            forward += jnp.dot(low, matrix, preferred_element_type=jnp.float32)
            inverse_ref[w, pl.ds(base, ROWS * GROUP)] = 1.0 / forward
            return c

        lax.fori_loop(0, SLABS // GROUP, blur, 0)


def back_kernel(
    shift_ref, offset_ref, other_ref, own_profile_ref, other_profile_ref, image_ref, inverse_ref,
    out_ref, b_ref, matrix_ref,
):
    upper, column, _ = place()
    row = lax.broadcasted_iota(jnp.int32, (1, 8, LENGTH), 1)

    for w in range(2):
        profile = jnp.where(upper == w, own_profile_ref[...], other_profile_ref[:, pl.ds(0, LENGTH)])
        matrix_ref[w] = blur_matrix(profile).astype(jnp.bfloat16)
        a, b = blend_of(column, w)

        def blur(k, c, w=w, a=a, b=b):
            base = pl.multiple_of(k * (ROWS * GROUP), ROWS * GROUP)
            edge = pl.multiple_of(lax.rem(base + TOTAL - 8, TOTAL), 8)
            slab = w * SLABS + lax.rem(k * GROUP + SLABS - 1, SLABS)
            image = image_ref[pl.ds(w * SLABS + k * GROUP, GROUP)].reshape(ROWS * GROUP, LENGTH)
            ratios = image.astype(jnp.float32) * inverse_ref[w, pl.ds(base, ROWS * GROUP)]
            before = image_ref[slab, pl.ds(ROWS - 8, 8)].astype(jnp.float32)
            before = before * inverse_ref[w, pl.ds(edge, 8)]
            wide = jnp.concatenate([before, ratios], axis=0)
            blended = a * ratios + b * wide[7 : ROWS * GROUP + 7]
            b_ref[w, pl.ds(base + 8, ROWS * GROUP)] = lax.dot_general(
                blended.astype(jnp.bfloat16),
                matrix_ref[w],
                (((1,), (1,)), ((), ())),
                preferred_element_type=jnp.float32,
            )
            return c

        lax.fori_loop(0, SLABS // GROUP, blur, 0)
        b_ref[w, pl.ds(0, 8)] = b_ref[w, pl.ds(TOTAL, 8)]
        b_ref[w, pl.ds(TOTAL + 8, 8)] = b_ref[w, pl.ds(8, 8)]

    views = []
    for w in range(2):
        is_own = upper == w
        shift = jnp.where(is_own, shift_ref[0], other_ref[0, LENGTH].astype(jnp.int32))
        offset = jnp.where(is_own, offset_ref[0], other_ref[0, LENGTH + 1].astype(jnp.int32))
        skip = lax.div(8 - offset, 8)
        rest = 8 - offset - 8 * skip
        views.append((shift, skip, rest, lax.rem(8 - rest, 8)))

    def join(k, c):
        for q in range(4):
            join_slab(4 * k + q)
        return c

    def join_slab(s):
        product = None
        for w, (shift, skip, rest, turn) in enumerate(views):
            t = lax.rem(s - shift + SLABS, SLABS)
            start = pl.multiple_of(t * ROWS + 8 * skip, 8)
            correction = tile_rows(b_ref[w, pl.ds(start, ROWS + 8)], rest, turn, row)
            product = correction if product is None else product * correction
        code = jnp.round(jnp.log(product) * PAIR_SCALE).astype(jnp.int32).astype(jnp.int16)
        for g in range(4):
            out_ref[lax.rem(g - column + 4, 4), s] = code[8 * g : 8 * g + 8]

    lax.fori_loop(0, SLABS // 4, join, 0)


def part_of(u, d):
    upper, column, _ = place()
    rows = pl.ds(pl.multiple_of(8 * lax.rem(column - d + 4, 4), 8), 8)
    lines = pl.ds(pl.multiple_of(32 * lax.rem(upper + u, 2), 32), 32)
    return rows, lines


def apply_codes(code_ref, est_ref, part_ref):
    logs = code_ref[...].astype(jnp.int32).astype(jnp.float32) * (1.0 / TOTAL_SCALE)
    part_ref[...] = est_ref[...] * jnp.exp(logs)


def first_kernel(places, later, est_ref, *refs):
    count = len(places)
    codes, (out_ref, rest_ref, parts_ref, in_sem, out_sem) = refs[:count], refs[count:]
    loads, stores = [], []
    for p, (u, d) in enumerate(places + later):
        rows, lines = part_of(u, d)
        target = parts_ref.at[p] if p < count else rest_ref.at[p - count]
        load = pltpu.make_async_copy(est_ref.at[rows, lines], target, in_sem.at[p])
        load.start()
        loads.append(load)
    for p, (u, d) in enumerate(places):
        rows, lines = part_of(u, d)
        loads[p].wait()
        apply_codes(codes[p], parts_ref.at[p], parts_ref.at[count + p])
        store = pltpu.make_async_copy(
            parts_ref.at[count + p], out_ref.at[rows, lines], out_sem.at[p]
        )
        store.start()
        stores.append(store)
    for copy in loads[count:] + stores:
        copy.wait()


def later_kernel(places, skip, est_ref, *refs):
    count = len(places)
    codes, (out_ref, parts_ref, sem) = refs[:count], refs[count + 1 :]
    stores = []
    for p, (u, d) in enumerate(places):
        rows, lines = part_of(u, d)
        apply_codes(codes[p], est_ref.at[skip + p], parts_ref.at[p])
        store = pltpu.make_async_copy(parts_ref.at[p], out_ref.at[rows, lines], sem.at[p])
        store.start()
        stores.append(store)
    for store in stores:
        store.wait()


def finish(places, estimate, pieces, early, middle):
    whole = jax.ShapeDtypeStruct((32, 64, LENGTH), jnp.float32)
    part = (8, 32, LENGTH)
    late = len(places) - early

    def cost(count):
        return pl.CostEstimate(
            flops=count << 17, bytes_accessed=count << 19, transcendentals=count << 16
        )

    result, rest = pl.pallas_call(
        functools.partial(first_kernel, places[:early], places[early:]),
        out_shape=(whole, jax.ShapeDtypeStruct((late, *part), jnp.float32)),
        in_specs=[ANY] + [VMEM] * early,
        out_specs=(ANY, VMEM),
        scratch_shapes=[
            pltpu.VMEM((2 * early, *part), jnp.float32),
            pltpu.SemaphoreType.DMA((early + late,)),
            pltpu.SemaphoreType.DMA((early,)),
        ],
        cost_estimate=cost(early),
        compiler_params=pltpu.CompilerParams(vmem_limit_bytes=16 << 20),
        name="first_kernel",
    )(estimate, *pieces[:early])
    for start, stop in ((early, early + middle), (early + middle, len(places))):
        count = stop - start
        result = pl.pallas_call(
            functools.partial(later_kernel, places[start:stop], start - early),
            out_shape=whole,
            in_specs=[VMEM] * (1 + count) + [ANY],
            out_specs=ANY,
            scratch_shapes=[
                pltpu.VMEM((count, *part), jnp.float32),
                pltpu.SemaphoreType.DMA((count,)),
            ],
            input_output_aliases={1 + count: 0},
            cost_estimate=cost(count),
            compiler_params=pltpu.CompilerParams(vmem_limit_bytes=16 << 20),
            name="later_kernel",
        )(rest, *pieces[start:stop], result)
    return result


def distance_route():
    route = []
    for v in range(8):
        for y in range(2):
            for z in range(8):
                for c in range(2):
                    target = 16 * y + 2 * ((z + v) % 8) + c
                    route.append((32 * v + 16 * y + 2 * z + c, 32 * v + target))
    return route


def swap_halves(block, axis, route, keep):
    mine = lax.dynamic_index_in_dim(block, keep, 0, keepdims=False)
    given = lax.dynamic_index_in_dim(block, 1 - keep, 0, keepdims=False)
    return mine, lax.ppermute(given, axis, route)


VMEM = pl.BlockSpec(memory_space=pltpu.VMEM)
SMEM = pl.BlockSpec(memory_space=pltpu.SMEM)
ANY = pl.BlockSpec(memory_space=pl.ANY)


def update(estimate, measured, blur_profile, view_offset, tile_shift):
    upper = lax.axis_index("upper")
    swap = [(0, 1), (1, 0)]
    moves = jnp.concatenate([tile_shift, view_offset]).astype(jnp.float32)
    info = jnp.concatenate([blur_profile, jnp.pad(moves, (0, 126))[None]], axis=1)
    other = lax.ppermute(info, "upper", swap)

    tile = lax.axis_index("tile")
    chip = pl.pallas_call(
        pick_kernel,
        out_shape=jax.ShapeDtypeStruct((2, 2, 2, ROWS, LENGTH), jnp.bfloat16),
        in_specs=[pl.BlockSpec(memory_space=pl.ANY)],
        out_specs=VMEM,
        scratch_shapes=[
            pltpu.VMEM((2, 2, 2, ROWS, 8, 128), jnp.float32),
            pltpu.SemaphoreType.DMA((2, 2, 2)),
        ],
        cost_estimate=pl.CostEstimate(flops=0, bytes_accessed=2 << 20, transcendentals=0),
        compiler_params=pltpu.CompilerParams(vmem_limit_bytes=32 << 19),
        name="pick_kernel",
    )(estimate)
    block = lax.ppermute(chip, ("upper", "column", "tile"), distance_route())
    image = measured[0].transpose(1, 0, 2)
    image_lines = lax.all_to_all(image, ("upper", "tile"), 0, 0, tiled=True)

    pair = swap_halves(block, "tile", [(i, i ^ 1) for i in range(32)], tile % 2)
    block = jnp.stack(pair, axis=2)
    own_line = lax.dynamic_index_in_dim(block, upper, 1, keepdims=False)
    other_line = lax.dynamic_index_in_dim(block, 1 - upper, 1, keepdims=False)
    far = lax.ppermute(other_line[1], ("upper", "tile"), [(i, i ^ 48) for i in range(64)])
    across = lax.ppermute(own_line[1], "tile", [(i, i ^ 16) for i in range(32)])
    beside = lax.ppermute(other_line[0], "upper", swap)
    piece = jnp.stack([own_line[0], across, beside, far]).reshape(2, 2, 2, ROWS, LENGTH)
    est_lines = [piece]
    for d in (1, 2, 3):
        route = [(i, (i + d) % 4) for i in range(4)]
        est_lines.append(lax.ppermute(piece, "column", route))

    inverse = pl.pallas_call(
        forward_kernel,
        out_shape=jax.ShapeDtypeStruct((2, TOTAL, LENGTH), jnp.float32),
        in_specs=[SMEM] * 3 + [VMEM] * 6,
        out_specs=VMEM,
        scratch_shapes=[pltpu.VMEM((TOTAL + 24, LENGTH), jnp.float32)],
        cost_estimate=pl.CostEstimate(
            flops=4 * TOTAL * LENGTH * LENGTH, bytes_accessed=8 << 20, transcendentals=0
        ),
        compiler_params=pltpu.CompilerParams(vmem_limit_bytes=16 << 20),
        name="forward_kernel",
    )(tile_shift, view_offset, other, blur_profile, other, *est_lines)
    codes = pl.pallas_call(
        back_kernel,
        out_shape=jax.ShapeDtypeStruct((4, SLABS, 8, LENGTH), jnp.int16),
        in_specs=[SMEM] * 3 + [VMEM] * 4,
        out_specs=VMEM,
        scratch_shapes=[
            pltpu.VMEM((2, TOTAL + 16, LENGTH), jnp.float32),
            pltpu.VMEM((2, LENGTH, LENGTH), jnp.bfloat16),
        ],
        compiler_params=pltpu.CompilerParams(vmem_limit_bytes=16 << 20),
        name="back_kernel",
    )(tile_shift, view_offset, other, blur_profile, other, image_lines, inverse)
    total = codes[0].astype(jnp.int32)
    for d in (2, 1, 3):
        route = [(i, (i + d) % 4) for i in range(4)]
        arrived = lax.ppermute(codes[d], "column", route)
        total += arrived.astype(jnp.int32)
    logs = ((total + 2) >> 2).astype(jnp.int16)
    logs = lax.all_to_all(logs, "tile", 0, 0, tiled=True)
    logs = logs.transpose(1, 0, 2)
    partner = lax.ppermute(logs, "upper", swap)
    places, pieces = [(0, 0), (1, 0)], [logs, partner]
    for u, d in [(0, 2), (0, 1), (0, 3), (1, 2), (1, 1), (1, 3)]:
        route = [(i, (i + d) % 4) for i in range(4)]
        places.append((u, d))
        pieces.append(lax.ppermute(pieces[u], "column", route))
    return finish(places, estimate, pieces, 4, 2)


def solution(mesh):
    fine = Mesh(mesh.devices.reshape(2, 4, 32), ("upper", "column", "tile"))
    view = ("upper", "column")
    placed = (P("tile"), P(view, "tile"), P(view), P(view), P(view))
    return jax.shard_map(update, mesh=fine, in_specs=placed, out_specs=P("tile"), check_vma=False)
```
